32 devices in a mesh: pool: 1, fsdp: 32 (over z, y, x, core).
Axes of the slice: x: 2, y: 2, z: 4, core: 2. Of those that a mesh axis runs over, the one named last changes fastest.
Arguments:
- noisy: bfloat16 [2048, 2560], P(('pool', 'fsdp')), may hold values from -6 to 6
- clean: bfloat16 [2048, 2560], P(('pool', 'fsdp')), may hold values from -6 to 6
- seg_ids: int32 [32], P('pool'), may hold values from 0 to 3, never falling along the last dimension, each value on 1 to 12 neighbouring positions
- lag_mask: int32 [32, 2], P(('pool', 'fsdp')), may hold values 0 or 1
- plan: int32 [32, 2], P(('pool', 'fsdp')), may hold values from 1 to 999, as said below
- w_query: bfloat16 [2560, 2560], P('fsdp'), may hold values from -0.125 to 0.125
- w_key: bfloat16 [2560, 2560], P('fsdp'), may hold values from -0.125 to 0.125
- time_proj: bfloat16 [128, 7680], replicated, may hold values from -0.5 to 0.5
- q_gain: float32 [2560], replicated, may hold values from 0.5 to 14
- k_gain: float32 [2560], replicated, may hold values from 0.5 to 14
Outputs:
- denoised: bfloat16 [2048, 2560], P(('pool', 'fsdp'))
The draws below stay inside these ranges and needn't reach their ends.
Inputs may be any that keep to these rules, and one draw needn't show every extreme that they name: seg_ids never falls along the spans; each rollout is 1 to 12 consecutive spans. `plan`: entry j of a row lies from 1000 * (1 - j) // 2 + 1 to 1000 * (2 - j) // 2 - 1, so each row falls strictly.
All inputs are finite; a program needn't handle non-finite values. No bound on the sum of `lag_mask` on one device may be relied on, other than what follows from the above.
Results may differ from the reference program's by a relative error of at most 0.024.
Values may be sent and summed in bfloat16 or wider, within the bound.
No kernel may reach another device: no remote copies, remote signals or barrier semaphores. Data moves between devices by JAX's collectives and lax.ppermute only.
A program may use at most 128 MiB of HBM per device.

```python
import math
import jax
import jax.numpy as jnp
import numpy as np
from jax import lax

D = 2560
HEADS = 20
HEAD_DIM = 128
TIME_FEAT = 128
ROWS = 64
STEPS = 2
LAGS = 2
LEVELS = 1000
MOST_SPANS = 12
SPANS = 32
ROLLOUTS = 4


def draw_plan(key, part):
    columns = []
    for level_index in range(STEPS):
        lowest = LEVELS * (STEPS - 1 - level_index) // STEPS + 1
        highest = LEVELS * (STEPS - level_index) // STEPS
        columns.append(jax.random.randint(jax.random.fold_in(key, level_index), (SPANS, 1), lowest, highest))
    return jnp.concatenate(columns, axis=1).astype(jnp.int32)


def gain_law(key):
    total_width = HEADS * HEAD_DIM
    result = jnp.exp(jax.random.uniform(key, (total_width,), jnp.float32, math.log(0.5), math.log(2.0)))
    return result.astype(jnp.float32)


def draw_q_gain(key, part):
    return gain_law(jax.random.fold_in(key, 11))


def draw_k_gain(key, part):
    return gain_law(jax.random.fold_in(key, 23))


def plant(values, own_key, low, high):
    longest = values.shape.index(max(values.shape))
    spots = []
    for shift in (0, 1):
        where = [jax.random.randint(jax.random.fold_in(own_key, axis), (), 0, length) for axis, length in enumerate(values.shape)]
        where[longest] = (where[longest] + shift) % values.shape[longest]
        spots.append(tuple(where))
    return values.at[spots[0]].set(low).at[spots[1]].set(high)


def block_levels(rng, extent, split, smallest, largest):
    level = 1.0
    for dim, blocks in split:
        draws = jax.random.uniform(jax.random.fold_in(jax.random.fold_in(rng, 6), dim), (blocks,), jnp.float32, smallest / len(split), largest / len(split))
        level = level * jnp.repeat(jnp.exp(draws), extent[dim] // blocks).reshape((-1,) + (1,) * (len(extent) - 1 - dim))
    return level


def length_profile(amount, total, most, slope):
    loads = [(1 << 20) // math.isqrt(standing ** slope) + 1 for standing in range(2, amount + 1)]
    rest, holding = total - most - (amount - 1), [1] * (amount - 1)
    while rest > 0:
        candidates = [i for i in range(amount - 1) if holding[i] < most]
        whole, remaining = sum([loads[i] for i in candidates]), rest
        for i in candidates:
            extra = min(most - holding[i], max(1, remaining * loads[i] // whole), rest)
            holding[i] = holding[i] + extra
            rest = rest - extra
    return np.array([most] + holding)


def ragged_sizes(stream_key, number_of, total, limit, skew):
    if number_of == 2:
        one = jax.random.randint(stream_key, (), max(1, total - limit), min(limit, total - 1) + 1)
        return jnp.stack([one, total - one])
    tallies = jnp.asarray(length_profile(number_of, total, limit, skew), jnp.int32)
    pairs = (number_of - 1) // 2
    donor, taker = tallies[1:1 + 2 * pairs:2], tallies[2:2 + 2 * pairs:2]
    slack = jnp.minimum(donor - 1, limit - taker)
    moved = jax.random.randint(jax.random.fold_in(stream_key, 1), (pairs,), 0, 1 << 20) % (slack + 1)
    tallies = tallies.at[1:1 + 2 * pairs:2].set(donor - moved).at[2:2 + 2 * pairs:2].set(taker + moved)
    return tallies[jax.random.permutation(jax.random.fold_in(stream_key, 2), number_of)]


def noise(key, extent, width, most, shards=(), kind=jnp.bfloat16):
    values = width * jax.random.normal(key, extent, jnp.float32)
    if shards:
        values = values * block_levels(key, extent, shards, -0.22, 0.18)
    return jnp.clip(values, -most, most).astype(kind)


def setup_inputs(seed: int = 0, part: int = 0) -> dict:
    splits = jax.random.split(jax.random.key(seed), 11)
    part_splits = jax.random.split(jax.random.fold_in(splits[10], part), 11)
    return {
        "noisy": noise(part_splits[0], (SPANS * ROWS, D), 1.0, 6.0, ((0, 32),)),
        "clean": noise(part_splits[1], (SPANS * ROWS, D), 1.0, 6.0, ((0, 32),)),
        "seg_ids": jnp.searchsorted(jnp.cumsum(ragged_sizes(part_splits[2], ROLLOUTS, SPANS, MOST_SPANS, 1)), jnp.arange(SPANS), side="right").astype(jnp.int32),
        "lag_mask": plant((jax.random.randint(part_splits[3], (SPANS, LAGS), 0, 4) < 3).astype(jnp.int32), jax.random.fold_in(part_splits[3], 1), 0, 1),
        "plan": draw_plan(jax.random.fold_in(jax.random.fold_in(splits[10], part), 71), part),
        "w_query": noise(splits[5], (D, HEADS * HEAD_DIM), D ** -0.5, 0.125, ((0, 32),)),
        "w_key": noise(splits[6], (D, HEADS * HEAD_DIM), D ** -0.5, 0.125, ((0, 32),)),
        "time_proj": noise(splits[7], (TIME_FEAT, 3 * D), TIME_FEAT ** -0.5, 0.5),
        "q_gain": draw_q_gain(jax.random.fold_in(splits[10], 71), part),
        "k_gain": draw_k_gain(jax.random.fold_in(splits[10], 71), part),
    }


SIGMA_SHIFT = 5.0
EPSILON = 1e-06
MASKED = -1e+30

def sigma_of(levels):
    fraction = levels.astype(jnp.float32) / LEVELS
    return SIGMA_SHIFT * fraction / (1.0 + (SIGMA_SHIFT - 1.0) * fraction)

def frequencies(half_count):
    return jnp.exp(-math.log(10000.0) * jnp.arange(half_count, dtype=jnp.float32) / half_count)

def modulation(sigmas, time_proj):
    half_count = time_proj.shape[0] // 2
    angles = 1000.0 * sigmas[:, None] * frequencies(half_count)[None, :]
    features = jnp.concatenate([jnp.cos(angles), jnp.sin(angles)], axis=1).astype(jnp.bfloat16)
    return jnp.dot(features, time_proj, preferred_element_type=jnp.float32)

def modulate(latent, shift_row, scale_row):
    values = latent.astype(jnp.float32)
    centred = values - lax.optimization_barrier(jnp.mean(values, axis=-1, keepdims=True))
    variance = lax.optimization_barrier(jnp.mean(centred * centred, axis=-1, keepdims=True))
    normed = centred * lax.rsqrt(variance + EPSILON)
    return (normed * (1.0 + scale_row) + shift_row).astype(jnp.bfloat16)

def normalize(values, gain):
    mean_square = lax.optimization_barrier(jnp.mean(values * values, axis=-1, keepdims=True))
    return values * lax.rsqrt(mean_square + EPSILON) * gain

def rotate(values, positions):
    half_count = HEAD_DIM // 2
    split_heads = values.reshape(values.shape[:-1] + (HEADS, HEAD_DIM))
    angles = positions[..., None] * frequencies(half_count)
    cosine = jnp.cos(angles)[..., None, :]
    sine = jnp.sin(angles)[..., None, :]
    front = split_heads[..., :half_count]
    back = split_heads[..., half_count:]
    turned = jnp.concatenate([front * cosine - back * sine, front * sine + back * cosine], axis=-1)
    return turned.reshape(values.shape)

def attend(operands):
    query_rows, key_rows, value_rows, usable = operands
    row_count = query_rows.shape[0]
    query_heads = query_rows.astype(jnp.float32).reshape(row_count, HEADS, HEAD_DIM)
    key_heads = key_rows.astype(jnp.float32).reshape(-1, HEADS, HEAD_DIM)
    value_heads = value_rows.astype(jnp.float32).reshape(-1, HEADS, HEAD_DIM)
    scores = jnp.einsum('qhd,khd->hqk', query_heads, key_heads) * HEAD_DIM ** (-0.5)
    scores = jnp.where(usable[None, None, :], scores, MASKED)
    highest = lax.optimization_barrier(jnp.max(scores, axis=-1, keepdims=True))
    expanded = jnp.exp(scores - highest)
    weights = (expanded / lax.optimization_barrier(jnp.sum(expanded, axis=-1, keepdims=True))).astype(jnp.bfloat16)
    mixed = jnp.einsum('hqk,khd->qhd', weights.astype(jnp.float32), value_heads)
    return mixed.reshape(row_count, HEADS * HEAD_DIM).astype(jnp.bfloat16)

def reference(noisy, clean, seg_ids, lag_mask, plan, w_query, w_key, time_proj, q_gain, k_gain):
    span_count = seg_ids.shape[0]
    order = jnp.arange(span_count, dtype=jnp.int32)
    segment_start = lax.optimization_barrier(jnp.sum((seg_ids[None, :] < seg_ids[:, None]).astype(jnp.int32), axis=1))
    span_place = order - segment_start
    positions = (span_place[:, None] * ROWS + jnp.arange(ROWS, dtype=jnp.int32)[None, :]).astype(jnp.float32)
    rest_mod = modulation(jnp.zeros((1,), jnp.float32), time_proj)[0]
    context_hidden = modulate(clean, rest_mod[:D], rest_mod[D:2 * D])
    context_key = rotate(normalize(jnp.dot(context_hidden, w_key, preferred_element_type=jnp.float32), k_gain).reshape(span_count, ROWS, -1), positions).astype(jnp.bfloat16)
    context_value = context_hidden.reshape(span_count, ROWS, -1)
    lag_keys = []
    lag_values = []
    usable_parts = [jnp.ones((span_count, ROWS), jnp.int32) > 0]
    for distance in range(1, LAGS + 1):
        source = jnp.maximum(order - distance, 0)
        allowed = (order >= distance) & (seg_ids[source] == seg_ids) & (lag_mask[:, distance - 1] == 1)
        lag_keys.append(context_key[source])
        lag_values.append(context_value[source])
        usable_parts.append(jnp.broadcast_to(allowed[:, None], (span_count, ROWS)))
    keys_context = jnp.concatenate(lag_keys, axis=1)
    values_context = jnp.concatenate(lag_values, axis=1)
    usable = jnp.concatenate(usable_parts, axis=1)
    sigmas = [sigma_of(plan[:, level_index]) for level_index in range(STEPS)] + [jnp.zeros((span_count,), jnp.float32)]
    latent = noisy
    for step_index in range(STEPS):
        mod_rows = modulation(sigmas[step_index], time_proj)
        current = latent.reshape(span_count, ROWS, D)
        hidden = modulate(current, mod_rows[:, None, :D], mod_rows[:, None, D:2 * D])
        flat_hidden = hidden.reshape(span_count * ROWS, D)
        query_all = rotate(normalize(jnp.dot(flat_hidden, w_query, preferred_element_type=jnp.float32), q_gain).reshape(span_count, ROWS, -1), positions).astype(jnp.bfloat16)
        key_all = rotate(normalize(jnp.dot(flat_hidden, w_key, preferred_element_type=jnp.float32), k_gain).reshape(span_count, ROWS, -1), positions).astype(jnp.bfloat16)
        keys_joined = jnp.concatenate([key_all, keys_context], axis=1)
        values_joined = jnp.concatenate([hidden, values_context], axis=1)
        mixed = lax.map(attend, (query_all, keys_joined, values_joined, usable))
        sigma_change = sigmas[step_index + 1] - sigmas[step_index]
        factor = sigma_change[:, None, None] * mod_rows[:, None, 2 * D:]
        latent = (current.astype(jnp.float32) + factor * mixed.astype(jnp.float32)).astype(jnp.bfloat16).reshape(span_count * ROWS, D)
    return latent
```

```python
import functools
import math

import jax
import jax.numpy as jnp
from jax import lax
from jax.experimental import pallas as pl
from jax.experimental.pallas import tpu as pltpu
from jax.sharding import PartitionSpec as P

HEADS = 20
HEAD_DIM = 128
STEPS = 2
LAGS = 2
LEVELS = 1000

SIGMA_SHIFT = 5.0
EPSILON = 1e-06
MASKED = -1e30
AXIS = "fsdp"


def sigma_of(levels):
    fraction = levels.astype(jnp.float32) / LEVELS
    return SIGMA_SHIFT * fraction / (1.0 + (SIGMA_SHIFT - 1.0) * fraction)


def frequencies(half_count):
    return jnp.exp(-math.log(10000.0) * jnp.arange(half_count, dtype=jnp.float32) / half_count)


def modulation(sigmas, time_proj):
    half_count = time_proj.shape[0] // 2
    angles = 1000.0 * sigmas[:, None] * frequencies(half_count)[None, :]
    features = jnp.concatenate([jnp.cos(angles), jnp.sin(angles)], axis=1).astype(jnp.bfloat16)
    return jnp.dot(features, time_proj, preferred_element_type=jnp.float32)


def modulate(latent, shift, scale):
    values = latent.astype(jnp.float32)
    centred = values - jnp.mean(values, axis=-1, keepdims=True)
    variance = jnp.mean(centred * centred, axis=-1, keepdims=True)
    normed = centred * lax.rsqrt(variance + EPSILON)
    return (normed * (1.0 + scale) + shift).astype(jnp.bfloat16)


def permute(value, target_of):
    pairs = [(s, target_of(s)) for s in range(lax.axis_size(AXIS))]
    return lax.ppermute(value, AXIS, [(s, t) for s, t in pairs if t is not None])


def swap_core(value):
    return permute(value, lambda s: s ^ 1)


def swap_x(value):
    return permute(value, lambda s: s ^ 2)


def swap_y(value):
    return permute(value, lambda s: s ^ 4)


def swap_z_pair(value):
    return permute(value, lambda s: s ^ 8)


def swap_z_middle(value):
    return permute(value, lambda s: {1: s + 8, 2: s - 8}.get(s // 8))


def z_outward(value):
    return permute(value, lambda s: {1: s - 8, 2: s + 8}.get(s // 8))


def gather_block(unit, device):
    rows, width = unit.shape
    half = rows // 2
    z = device // 8
    y = (device // 4) % 2
    x = (device // 2) % 2
    middle = (z == 1) | (z == 2)
    pair = swap_z_pair(unit)
    across = swap_z_middle(unit)
    two_mid = swap_z_middle(pair)
    two_end = z_outward(across)
    three_end = z_outward(two_mid)
    slots = [
        unit,
        pair,
        jnp.where(middle, two_mid, two_end),
        jnp.where(middle, across, three_end),
    ]
    planes = []
    for step, own in enumerate(slots):
        from_x = swap_x(own)
        from_y = swap_y(own)
        far_low = swap_y(from_x[:half])
        far_high = swap_x(from_y[half:])
        far = jnp.concatenate([far_low, far_high], axis=0)
        plane = jnp.zeros((4, rows, width), unit.dtype)
        place = y * 2 + x
        for piece, at in ((own, place), (from_x, place ^ 1), (from_y, place ^ 2), (far, place ^ 3)):
            plane = lax.dynamic_update_slice(plane, piece[None], (at, 0, 0))
        planes.append((z ^ step, plane.reshape(4 * rows, width)))
    return planes


def gather_any(unit, device):
    size = lax.axis_size(AXIS)
    groups = [list(range(core, size, 2)) for core in range(2)]
    return [(jnp.int32(0), lax.all_gather(unit, AXIS, axis=0, tiled=True, axis_index_groups=groups))]


def turn(values, cosine, sine):
    return values * cosine + pltpu.roll(values, HEAD_DIM // 2, 1) * sine


def attend_body(first, *refs):
    if first:
        (q_ref, k_ref, c_ref, qs_ref, ks_ref, cs_ref, qg_ref, kg_ref, cos_ref, sin_ref, mask_ref,
         v_ref, cv_ref, lat_ref, fac_ref, out_ref, ck_ref) = refs
    else:
        (q_ref, k_ref, c_ref, qs_ref, ks_ref, qg_ref, kg_ref, cos_ref, sin_ref, mask_ref,
         v_ref, cv_ref, lat_ref, fac_ref, out_ref) = refs
    rows = q_ref.shape[0]
    extra = c_ref.shape[0]
    own_cos, own_sin = cos_ref[extra - rows // 2 :, :], sin_ref[extra - rows // 2 :, :]
    query = turn(q_ref[...] * qs_ref[...] * qg_ref[...], own_cos, own_sin).astype(jnp.bfloat16)
    key = turn(k_ref[...] * ks_ref[...] * kg_ref[...], own_cos, own_sin).astype(jnp.bfloat16)
    if first:
        past = turn(
            c_ref[...] * cs_ref[...] * kg_ref[...], cos_ref[:extra, :], sin_ref[:extra, :]
        ).astype(jnp.bfloat16)
        ck_ref[...] = past
    else:
        past = c_ref[...]
    keys = jnp.concatenate([key, past], axis=0)
    values = jnp.concatenate([v_ref[...], cv_ref[...]], axis=0)
    scores = lax.dot_general(
        query, keys, (((1,), (1,)), ((), ())), preferred_element_type=jnp.float32
    ) * HEAD_DIM ** (-0.5)
    scores = jnp.where(mask_ref[...] > 0.0, scores, MASKED)
    expanded = jnp.exp(scores - jnp.max(scores, axis=-1, keepdims=True))
    weights = (expanded / jnp.sum(expanded, axis=-1, keepdims=True)).astype(jnp.bfloat16)
    mixed = jnp.dot(weights, values, preferred_element_type=jnp.float32).astype(jnp.bfloat16)
    factor = jnp.concatenate(
        [jnp.broadcast_to(fac_ref[i : i + 1, :], (rows // 2, HEAD_DIM)) for i in range(2)], axis=0
    )
    out_ref[...] = (
        lat_ref[...].astype(jnp.float32) + factor * mixed.astype(jnp.float32)
    ).astype(jnp.bfloat16)


def attend(first, raw, past, scales, gains, tables, mask, values, past_values, latent, factor):
    rows, width = latent.shape
    extra = past.shape[0]
    heads = width // HEAD_DIM

    def column(count, shift=0):
        return pl.BlockSpec((count, HEAD_DIM), lambda h: (0, h + shift))

    def whole(array):
        return pl.BlockSpec(array.shape, lambda h: (0, 0))

    operands = [raw, raw, past, *scales, *gains, *tables, mask, values, past_values, latent, factor]
    specs = [column(rows), column(rows, heads), column(extra)]
    specs += [whole(s) for s in scales]
    specs += [column(1), column(1)]
    specs += [whole(t) for t in tables] + [whole(mask)]
    specs += [column(rows), column(extra), column(rows), column(factor.shape[0])]
    shapes = [jax.ShapeDtypeStruct((rows, width), jnp.bfloat16)]
    outs = [column(rows)]
    if first:
        shapes.append(jax.ShapeDtypeStruct((extra, width), jnp.bfloat16))
        outs.append(column(extra))
    return pl.pallas_call(
        functools.partial(attend_body, first),
        grid=(heads,),
        in_specs=specs,
        out_specs=outs,
        out_shape=shapes,
        name="attend",
    )(*operands)


def local(noisy, clean, seg_ids, lag_mask, plan, w_query, w_key, time_proj, q_gain, k_gain):
    rows, width = noisy.shape
    inner = w_query.shape[1]
    half = inner // 2
    shard = w_query.shape[0]
    devices = lax.axis_size(AXIS)
    device = lax.axis_index(AXIS)
    core = device % 2
    first_span = device - core
    is_low = core == 0

    def mine(value, axis):
        return lax.dynamic_slice_in_dim(value, core * half, half, axis)

    def theirs(value, axis):
        return lax.dynamic_slice_in_dim(value, (1 - core) * half, half, axis)

    def in_order(own, other, axis):
        low = jnp.where(is_low, own, other)
        high = jnp.where(is_low, other, own)
        return jnp.concatenate([low, high], axis=axis)

    own_rows = jnp.concatenate([mine(w_query, 1), mine(w_key, 1)], axis=1)
    sent_rows = jnp.concatenate([theirs(w_query, 1), theirs(w_key, 1)], axis=1)
    unit = in_order(own_rows, swap_core(sent_rows), 0)
    planes = (gather_block if devices == 32 else gather_any)(unit, device)
    plane_rows = planes[0][1].shape[0]
    plane_count = width // plane_rows

    noisy_both = in_order(noisy, swap_core(noisy), 0)
    before = permute(clean, lambda s: s + 2 if s + 2 < devices else None)
    before_both = in_order(before, swap_core(before), 0)
    first_clean = jnp.where(is_low, clean, swap_core(clean))
    past_clean = jnp.concatenate([before_both, first_clean], axis=0)
    small = jnp.concatenate([plan, lag_mask], axis=1)
    small_both = in_order(small, swap_core(small), 0)
    plan_both, lags_both = small_both[:, :STEPS], small_both[:, STEPS:]

    sigmas = [sigma_of(plan_both[:, j]) for j in range(STEPS)] + [jnp.zeros((2,), jnp.float32)]
    mods = modulation(jnp.concatenate([jnp.zeros((1,), jnp.float32)] + sigmas[:STEPS]), time_proj)

    def per_row(pair):
        return jnp.repeat(pair, rows, axis=0)

    step_mods = [mods[1 + 2 * j : 3 + 2 * j] for j in range(STEPS)]
    factors = [
        (sigmas[j + 1] - sigmas[j])[:, None] * mine(step_mods[j][:, 2 * width :], 1)
        for j in range(STEPS)
    ]
    past_hidden = modulate(past_clean, mods[:1, :width], mods[:1, width : 2 * width])
    hidden = modulate(
        noisy_both, per_row(step_mods[0][:, :width]), per_row(step_mods[0][:, width : 2 * width])
    )

    spans = jnp.maximum(first_span - 2 + jnp.arange(4, dtype=jnp.int32), 0)
    segments = seg_ids[spans]
    starts = jnp.sum((seg_ids[None, :] < segments[:, None]).astype(jnp.int32), axis=1)
    positions = (
        (spans - starts)[:, None] * rows + jnp.arange(rows, dtype=jnp.int32)[None, :]
    ).astype(jnp.float32).reshape(-1, 1)
    angles = positions * frequencies(HEAD_DIM // 2)[None, :]
    cosine = jnp.concatenate([jnp.cos(angles)] * 2, axis=1)
    sine = jnp.concatenate([-jnp.sin(angles), jnp.sin(angles)], axis=1)
    allowed = []
    for local_span in range(2):
        seen = [jnp.bool_(s == local_span) for s in range(2)]
        for source in range(3):
            lag = local_span + 2 - source
            if 1 <= lag <= LAGS:
                usable = (
                    (first_span + local_span >= lag)
                    & (segments[source] == segments[2 + local_span])
                    & (lags_both[local_span, lag - 1] == 1)
                )
            else:
                usable = jnp.bool_(False)
            seen.append(usable)
        allowed.append(jnp.stack(seen))
    mask = jnp.repeat(jnp.repeat(jnp.stack(allowed).astype(jnp.float32), rows, 0), rows, 1)

    def project(values, columns):
        total = None
        for place, weights in planes:
            part = lax.dynamic_slice_in_dim(values, place * plane_rows, plane_rows, 1)
            part = jnp.dot(part, weights[:, columns], preferred_element_type=jnp.float32)
            total = part if total is None else total + part
        return total

    def squares(values):
        return jnp.sum(values * values, axis=-1)

    def scale_of(total):
        return lax.rsqrt(total / inner + EPSILON)[:, None]

    gains = (mine(q_gain, 0)[None, :], mine(k_gain, 0)[None, :])
    tables = (cosine, sine)
    latent = mine(noisy_both, 1)
    values = mine(hidden, 1)
    past_values = mine(past_hidden, 1)

    raw = project(hidden, slice(0, 2 * half))
    past_raw = project(past_hidden, slice(half, 2 * half))
    sums = jnp.concatenate([squares(raw[:, :half]), squares(raw[:, half:]), squares(past_raw)])
    scale = scale_of(sums + swap_core(sums))
    both = 2 * rows
    latent, past_key = attend(
        True, raw, past_raw, (scale[:both], scale[both : 2 * both], scale[2 * both :]),
        gains, tables, mask, values, past_values, latent, factors[0],
    )

    f32 = latent.astype(jnp.float32)
    half_mean = jnp.mean(f32, axis=-1)
    half_centred = f32 - half_mean[:, None]
    moments = jnp.stack([half_mean, jnp.sum(half_centred * half_centred, axis=-1)])
    others = swap_core(moments)
    mean = 0.5 * (moments[0] + others[0])
    gap = moments[0] - others[0]
    variance = (moments[1] + others[1] + gap * gap * (half / 2)) / inner
    normed = (f32 - mean[:, None]) * lax.rsqrt(variance + EPSILON)[:, None]
    shift = per_row(mine(step_mods[1][:, :width], 1))
    gain = per_row(mine(step_mods[1][:, width : 2 * width], 1))
    values = (normed * (1.0 + gain) + shift).astype(jnp.bfloat16)
    hidden = in_order(values, swap_core(values), 1)

    raw = project(hidden, slice(0, 2 * half))
    sums = jnp.concatenate([squares(raw[:, :half]), squares(raw[:, half:])])
    scale = scale_of(sums + swap_core(sums))
    (latent,) = attend(
        False, raw, past_key, (scale[:both], scale[both:]),
        gains, tables, mask, values, past_values, latent, factors[1],
    )
    kept = lax.dynamic_slice_in_dim(latent, core * rows, rows, 0)
    sent = lax.dynamic_slice_in_dim(latent, (1 - core) * rows, rows, 0)
    return in_order(kept, swap_core(sent), 1)


def solution(mesh):
    placed = (
        P(("pool", "fsdp"), None),
        P(("pool", "fsdp"), None),
        P("pool"),
        P(("pool", "fsdp"), None),
        P(("pool", "fsdp"), None),
        P("fsdp", None),
        P("fsdp", None),
        P(),
        P(),
        P(),
    )
    return jax.shard_map(
        local, mesh=mesh, in_specs=placed, out_specs=P(("pool", "fsdp"), None), check_vma=False
    )
```

```python
import functools
import math

import jax
import jax.numpy as jnp
from jax import lax
from jax.experimental import pallas as pl
from jax.experimental.pallas import tpu as pltpu
from jax.sharding import PartitionSpec as P


HEAD_DIM = 128
STEPS = 2
LAGS = 2
LEVELS = 1000

SIGMA_SHIFT = 5.0
EPSILON = 1e-06
MASKED = -1e30
AXIS = "fsdp"


def sigma_of(levels):
    fraction = levels.astype(jnp.float32) / LEVELS
    return SIGMA_SHIFT * fraction / (1.0 + (SIGMA_SHIFT - 1.0) * fraction)


def frequencies(half_count):
    return jnp.exp(-math.log(10000.0) * jnp.arange(half_count, dtype=jnp.float32) / half_count)


def modulation(sigmas, time_proj):
    half_count = time_proj.shape[0] // 2
    angles = 1000.0 * sigmas[:, None] * frequencies(half_count)[None, :]
    features = jnp.concatenate([jnp.cos(angles), jnp.sin(angles)], axis=1).astype(jnp.bfloat16)
    return jnp.dot(features, time_proj, preferred_element_type=jnp.float32)


def modulate(latent, shift, scale):
    parts = shift.shape[0]
    values = latent.astype(jnp.float32).reshape(parts, -1, latent.shape[1])
    centred = values - jnp.mean(values, axis=-1, keepdims=True)
    variance = jnp.mean(centred * centred, axis=-1, keepdims=True)
    normed = centred * lax.rsqrt(variance + EPSILON)
    result = normed * (1.0 + scale[:, None, :]) + shift[:, None, :]
    return result.astype(jnp.bfloat16).reshape(latent.shape)


def permute(value, target_of):
    pairs = [(s, target_of(s)) for s in range(lax.axis_size(AXIS))]
    return lax.ppermute(value, AXIS, [(s, t) for s, t in pairs if t is not None])


def swap_core(value):
    return permute(value, lambda s: s ^ 1)


def swap_x(value):
    return permute(value, lambda s: s ^ 2)


def swap_y(value):
    return permute(value, lambda s: s ^ 4)


def swap_z_pair(value):
    return permute(value, lambda s: s ^ 8)


def swap_z_middle(value):
    return permute(value, lambda s: {1: s + 8, 2: s - 8}.get(s // 8))


def z_outward(value):
    return permute(value, lambda s: {1: s - 8, 2: s + 8}.get(s // 8))


def across_plane(value):
    half = value.shape[0] // 2
    from_x = swap_x(value)
    from_y = swap_y(value)
    low, high = from_x[:half], from_y[half:]
    return [value, from_x, from_y, swap_y(low), swap_x(high)]


def across_plane_in_halves(value):
    half = value.shape[0] // 2
    low, high = value[:half], value[half:]
    low_x = swap_x(low)
    high_y = swap_y(high)
    high_x = swap_x(high)
    low_y = swap_y(low)
    return [value, low_x, high_x, low_y, high_y, swap_y(low_x), swap_x(high_y)]


def gather_block(unit, device):
    z = device // 8
    place = (device // 2) % 4
    middle = (z == 1) | (z == 2)
    pair = swap_z_pair(unit)
    across = swap_z_middle(unit)
    two_mid = swap_z_middle(pair)
    two_end = z_outward(across)
    second = jnp.where(middle, two_mid, two_end)
    three_end = z_outward(second)
    third = jnp.where(middle, across, three_end)
    slots = [unit, pair, second, third]
    pieces = [across_plane(slot) for slot in slots[:3]]
    pieces.append(across_plane_in_halves(third))
    rows = unit.shape[0]
    halves = [[(i, 0, rows // 2), (i, rows // 2, rows // 2)] for i in range(4)]
    spots = [[(0, 0, rows), (1, 0, rows), (2, 0, rows)] + halves[3]] * 3
    spots.append([(0, 0, rows)] + halves[1] + halves[2] + halves[3])
    return [z ^ step for step in range(4)], place, pieces, spots


def gather_any(unit, device):
    size = lax.axis_size(AXIS)
    groups = [list(range(core, size, 2)) for core in range(2)]
    whole = lax.all_gather(unit, AXIS, axis=0, tiled=True, axis_index_groups=groups)
    none = jnp.int32(0)
    return [none], none, [[whole]], [[(0, 0, whole.shape[0])]]


def absorb_body(spots, step, has_sum, last, places_ref, hidden_ref, *refs):
    count = len(spots)
    piece_refs, refs = refs[:count], refs[count:]
    if has_sum:
        raw_in_ref, past_in_ref, *refs = refs
    plane_out_ref, raw_ref, past_ref, *refs = refs
    if last:
        sum_ref, *refs = refs
    plane_ref, sems, out_sem = refs
    place = places_ref[places_ref.shape[0] - 2]
    copies = []
    for i, (other, start, size) in enumerate(spots):
        target = plane_ref.at[jnp.bitwise_xor(place, other), pl.ds(start, size), :]
        copies.append(pltpu.make_async_copy(piece_refs[i], target, sems.at[i]))
    for copy in copies:
        copy.start()
    for copy in copies:
        copy.wait()
    out = pltpu.make_async_copy(plane_ref, plane_out_ref, out_sem)
    out.start()
    weights = plane_ref[...].reshape(-1, plane_ref.shape[2])
    hidden = hidden_ref[places_ref[step]]
    rows, split = raw_ref.shape[0], weights.shape[1] // 2
    raw = jnp.dot(hidden[:rows], weights, preferred_element_type=jnp.float32)
    past = jnp.dot(hidden[rows:], weights[:, split:], preferred_element_type=jnp.float32)
    if has_sum:
        raw = raw + raw_in_ref[...]
        past = past + past_in_ref[...]
    raw_ref[...] = raw
    past_ref[...] = past
    if last:
        at = 0
        for side in (raw[:, :split], raw[:, split:], past):
            count = side.shape[0]
            total = jnp.sum(side * side, -1, keepdims=True)
            sum_ref[at : at + count] = jnp.broadcast_to(total, (count, HEAD_DIM))
            at += count
    out.wait()


def absorb(step, last, places, hidden, pieces, spots, chips, rows, sums):
    hbm = pl.BlockSpec(memory_space=pltpu.HBM)
    vmem = pl.BlockSpec(memory_space=pltpu.VMEM)
    width = pieces[0].shape[1]
    chip_rows = hidden.shape[2] // chips
    past_rows = hidden.shape[1] - rows
    operands = [places, hidden, *pieces, *sums]
    specs = [pl.BlockSpec(memory_space=pltpu.SMEM), vmem] + [hbm] * len(pieces)
    specs += [vmem] * len(sums)
    shapes = [
        pltpu.HBM((chips, chip_rows, width), jnp.bfloat16),
        jax.ShapeDtypeStruct((rows, width), jnp.float32),
        jax.ShapeDtypeStruct((past_rows, width // 2), jnp.float32),
    ]
    outs = [hbm, vmem, vmem]
    if last:
        shapes.append(jax.ShapeDtypeStruct((2 * rows + past_rows, HEAD_DIM), jnp.float32))
        outs.append(vmem)
    return pl.pallas_call(
        functools.partial(absorb_body, spots, step, bool(sums), last),
        in_specs=specs,
        out_specs=outs,
        out_shape=shapes,
        scratch_shapes=[
            pltpu.VMEM((chips, chip_rows, width), jnp.bfloat16),
            pltpu.SemaphoreType.DMA((len(pieces),)),
            pltpu.SemaphoreType.DMA,
        ],
        compiler_params=pltpu.CompilerParams(vmem_limit_bytes=16 << 20),
        name="absorb",
    )(*operands)


def turn(values, cosine, sine):
    return values * cosine + pltpu.roll(values, HEAD_DIM // 2, 1) * sine


def attend_body(first, inner, *refs):
    (raw_ref, own_sum_ref, other_sum_ref, q_gain_ref, k_gain_ref, cos_ref, sin_ref,
     usable_ref, v_ref, past_v_ref, latent_ref, factor_ref, *refs) = refs
    if first:
        past_ref, out_ref, past_key_ref = refs
    else:
        past_key_ref, out_ref = refs
    rows, width = latent_ref.shape
    extra = past_v_ref.shape[0]
    heads = width // HEAD_DIM
    scale = lax.rsqrt((own_sum_ref[...] + other_sum_ref[...]) / inner + EPSILON)
    q_scale, k_scale = scale[:rows], scale[rows : 2 * rows]
    turned = slice(extra - rows // 2, extra + rows // 2)
    own_cos, own_sin = cos_ref[turned, :], sin_ref[turned, :]

    def per_row(pair):
        rows_of = [jnp.broadcast_to(pair[i : i + 1], (rows // 2, pair.shape[1])) for i in range(2)]
        return jnp.concatenate(rows_of, axis=0)

    allowed = per_row(usable_ref[...]) > 0.0
    for head in range(heads):
        at = slice(head * HEAD_DIM, (head + 1) * HEAD_DIM)
        key_at = slice(width + at.start, width + at.stop)
        query = raw_ref[:, at] * q_scale * q_gain_ref[:, at]
        query = turn(query, own_cos, own_sin).astype(jnp.bfloat16)
        key = raw_ref[:, key_at] * k_scale * k_gain_ref[:, at]
        key = turn(key, own_cos, own_sin).astype(jnp.bfloat16)
        if first:
            past = past_ref[:, at] * scale[2 * rows :] * k_gain_ref[:, at]
            past = turn(past, cos_ref[:extra, :], sin_ref[:extra, :]).astype(jnp.bfloat16)
            past_key_ref[:, at] = past
        else:
            past = past_key_ref[:, at]
        keys = jnp.concatenate([key, past], axis=0)
        values = jnp.concatenate([v_ref[:, at], past_v_ref[:, at]], axis=0)
        scores = lax.dot_general(
            query, keys, (((1,), (1,)), ((), ())), preferred_element_type=jnp.float32
        ) * HEAD_DIM ** (-0.5)
        scores = jnp.where(allowed, scores, MASKED)
        expanded = jnp.exp(scores - jnp.max(scores, axis=-1, keepdims=True))
        weights = (expanded / jnp.sum(expanded, axis=-1, keepdims=True)).astype(jnp.bfloat16)
        mixed = jnp.dot(weights, values, preferred_element_type=jnp.float32).astype(jnp.bfloat16)
        step = per_row(factor_ref[:, at]) * mixed.astype(jnp.float32)
        out_ref[:, at] = (latent_ref[:, at].astype(jnp.float32) + step).astype(jnp.bfloat16)


def attend(first, inner, raw, sums, others, gains, tables, fixed, latent, factor, past):
    shapes = [jax.ShapeDtypeStruct(latent.shape, jnp.bfloat16)]
    if first:
        shapes.append(jax.ShapeDtypeStruct(past.shape, jnp.bfloat16))
    return pl.pallas_call(
        functools.partial(attend_body, first, inner),
        out_shape=shapes,
        compiler_params=pltpu.CompilerParams(vmem_limit_bytes=16 << 20),
        name="attend",
    )(raw, sums, others, *gains, *tables, *fixed, latent, factor, past)


def project_body(places_ref, own_ref, other_ref, mod_ref, *refs):
    count = len(refs) - 6
    plane_refs = refs[:count]
    raw_ref, sum_ref, value_ref, hidden_ref, weight_ref, sems = refs[count:]
    rows, half = own_ref.shape
    parts, _, part_width = hidden_ref.shape
    copies = [
        pltpu.make_async_copy(ref, weight_ref.at[i], sems.at[i])
        for i, ref in enumerate(plane_refs)
    ]
    for copy in copies:
        copy.start()
    is_low = places_ref[count + 1] == 0
    own, other = own_ref[...].astype(jnp.float32), other_ref[...].astype(jnp.float32)
    low, high = jnp.where(is_low, own, other), jnp.where(is_low, other, own)
    width = 2 * half
    mean = (jnp.sum(low, -1, keepdims=True) + jnp.sum(high, -1, keepdims=True)) / width
    low, high = low - mean, high - mean
    variance = (
        jnp.sum(low * low, -1, keepdims=True) + jnp.sum(high * high, -1, keepdims=True)
    ) / width
    scale = lax.rsqrt(variance + EPSILON)
    sides = []
    for side, centred in enumerate((low, high)):
        normed = centred * scale
        at = slice(side * half, (side + 1) * half)
        gain_at = slice(width + side * half, width + (side + 1) * half)
        pieces = []
        for span in range(2):
            piece = normed[span * (rows // 2) : (span + 1) * (rows // 2)]
            row = slice(3 + span, 4 + span)
            pieces.append(piece * (1.0 + mod_ref[row, gain_at]) + mod_ref[row, at])
        sides.append(jnp.concatenate(pieces, axis=0).astype(jnp.bfloat16))
    value_ref[...] = jnp.where(is_low, sides[0], sides[1])
    for i in range(parts):
        for side in range(2):
            if parts == 1:
                hidden_ref[0, :, side * half : (side + 1) * half] = sides[side]
            elif i * part_width // half == side:
                at = i * part_width - side * half
                hidden_ref[i] = sides[side][:, at : at + part_width]
    total = None
    for i, copy in enumerate(copies):
        copy.wait()
        weights = weight_ref[i].reshape(-1, weight_ref.shape[-1])
        part = jnp.dot(hidden_ref[places_ref[i]], weights, preferred_element_type=jnp.float32)
        total = part if total is None else total + part
    raw_ref[...] = total
    for i in range(2):
        side = total[:, i * half : (i + 1) * half]
        square = jnp.sum(side * side, -1, keepdims=True)
        sum_ref[i * rows : (i + 1) * rows] = jnp.broadcast_to(square, (rows, HEAD_DIM))


def project_latent(places, own, other, mods, planes):
    rows, half = own.shape
    count = len(planes)
    planes = [pltpu.with_memory_space_constraint(plane, pltpu.HBM) for plane in planes]
    vmem = pl.BlockSpec(memory_space=pltpu.VMEM)
    hbm = pl.BlockSpec(memory_space=pltpu.HBM)
    return pl.pallas_call(
        project_body,
        in_specs=[pl.BlockSpec(memory_space=pltpu.SMEM)] + [vmem] * 3 + [hbm] * count,
        out_shape=[
            jax.ShapeDtypeStruct((rows, planes[0].shape[-1]), jnp.float32),
            jax.ShapeDtypeStruct((2 * rows, HEAD_DIM), jnp.float32),
            jax.ShapeDtypeStruct((rows, half), jnp.bfloat16),
        ],
        scratch_shapes=[
            pltpu.VMEM((count, rows, 2 * half // count), jnp.bfloat16),
            pltpu.VMEM((count,) + planes[0].shape, jnp.bfloat16),
            pltpu.SemaphoreType.DMA((count,)),
        ],
        compiler_params=pltpu.CompilerParams(vmem_limit_bytes=24 << 20),
        name="project",
    )(places, own, other, mods, *planes)


def denoise(noisy, clean, seg_ids, lag_mask, plan, w_query, w_key, time_proj, q_gain, k_gain):
    rows, width = noisy.shape
    inner = w_query.shape[1]
    half = inner // 2
    devices = lax.axis_size(AXIS)
    device = lax.axis_index(AXIS)
    core = device % 2
    first_span = device - core
    is_low = core == 0

    def mine(value, axis):
        return lax.dynamic_slice_in_dim(value, core * half, half, axis)

    def theirs(value, axis):
        return lax.dynamic_slice_in_dim(value, (1 - core) * half, half, axis)

    def in_order(own, other, axis):
        low = jnp.where(is_low, own, other)
        high = jnp.where(is_low, other, own)
        return jnp.concatenate([low, high], axis=axis)

    before = permute(clean, lambda s: s + 2 if s + 2 < devices else None)
    others = swap_core(clean)

    own_rows = jnp.concatenate([mine(w_query, 1), mine(w_key, 1)], axis=1)
    sent_rows = jnp.concatenate([theirs(w_query, 1), theirs(w_key, 1)], axis=1)
    unit = in_order(own_rows, swap_core(sent_rows), 0)
    unit, noisy, seg_ids, plan, lag_mask, time_proj = lax.optimization_barrier(
        (unit, noisy, seg_ids, plan, lag_mask, time_proj)
    )
    gather = gather_block if devices == 32 else gather_any
    plane_ids, place, pieces, spots = gather(unit, device)
    noisy_both = in_order(noisy, swap_core(noisy), 0)
    small = jnp.concatenate([plan, lag_mask], axis=1)
    small_both = in_order(small, swap_core(small), 0)
    plan_both, lags_both = small_both[:, :STEPS], small_both[:, STEPS:]
    sigmas = [sigma_of(plan_both[:, j]) for j in range(STEPS)] + [jnp.zeros((2,), jnp.float32)]
    mods = modulation(jnp.concatenate([jnp.zeros((1,), jnp.float32)] + sigmas[:STEPS]), time_proj)
    step_mods = [mods[1 + 2 * j : 3 + 2 * j] for j in range(STEPS)]
    hidden = modulate(noisy_both, step_mods[0][:, :width], step_mods[0][:, width : 2 * width])
    latent = mine(noisy_both, 1)
    values = mine(hidden, 1)

    before_both = in_order(before, swap_core(before), 0)
    past_clean = jnp.concatenate([before_both, jnp.where(is_low, clean, others)], axis=0)
    past_hidden = modulate(past_clean, mods[:1, :width], mods[:1, width : 2 * width])
    past_values = mine(past_hidden, 1)
    stack = jnp.concatenate([hidden, past_hidden], axis=0)
    stack = stack.reshape(stack.shape[0], len(plane_ids), -1).swapaxes(0, 1)
    places = jnp.stack(plane_ids + [place, core]).astype(jnp.int32)

    factors = [
        (sigmas[j + 1] - sigmas[j])[:, None] * mine(step_mods[j][:, 2 * width :], 1)
        for j in range(STEPS)
    ]
    gains = (mine(q_gain, 0)[None, :], mine(k_gain, 0)[None, :])
    spans = jnp.maximum(first_span - 2 + jnp.arange(4, dtype=jnp.int32), 0)
    segments = seg_ids[spans]
    starts = jnp.sum((seg_ids[None, :] < segments[:, None]).astype(jnp.int32), axis=1)
    positions = (
        (spans - starts)[:, None] * rows + jnp.arange(rows, dtype=jnp.int32)[None, :]
    ).astype(jnp.float32).reshape(-1, 1)
    angles = positions * frequencies(HEAD_DIM // 2)[None, :]
    cosine = jnp.concatenate([jnp.cos(angles)] * 2, axis=1)
    sine = jnp.concatenate([-jnp.sin(angles), jnp.sin(angles)], axis=1)
    tables = (cosine, sine)
    block = jnp.arange(5 * rows, dtype=jnp.int32)[None, :] // rows
    here = jnp.arange(2, dtype=jnp.int32)[:, None]
    usable = block == here
    for lag in range(1, LAGS + 1):
        allowed = (
            (first_span + here >= lag)
            & (segments[2 - lag : 4 - lag] == segments[2:])[:, None]
            & (lags_both[:, lag - 1 : lag] == 1)
        )
        usable = usable | (allowed & (block == here + 4 - lag))
    usable = usable.astype(jnp.float32)

    chips = 4 if len(pieces) == 4 else 1
    sums, planes = [], []
    for step, parts in enumerate(pieces):
        last = step + 1 == len(pieces)
        plane, *sums = absorb(step, last, places, stack, parts, spots[step], chips, 2 * rows, sums)
        planes.append(plane)
    raw, past_raw, sums = sums
    latent, past_key = attend(
        True, inner, raw, sums, swap_core(sums), gains, tables, (usable, values, past_values),
        latent, factors[0], past_raw,
    )
    raw, sums, values = project_latent(places, latent, swap_core(latent), mods, planes)
    (latent,) = attend(
        False, inner, raw, sums, swap_core(sums), gains, tables, (usable, values, past_values),
        latent, factors[1], past_key,
    )
    kept = lax.dynamic_slice_in_dim(latent, core * rows, rows, 0)
    sent = lax.dynamic_slice_in_dim(latent, (1 - core) * rows, rows, 0)
    return in_order(kept, swap_core(sent), 1)


def solution(mesh):
    placed = (
        P(("pool", "fsdp"), None),
        P(("pool", "fsdp"), None),
        P("pool"),
        P(("pool", "fsdp"), None),
        P(("pool", "fsdp"), None),
        P("fsdp", None),
        P("fsdp", None),
        P(),
        P(),
        P(),
    )
    return jax.shard_map(
        denoise, mesh=mesh, in_specs=placed, out_specs=P(("pool", "fsdp"), None), check_vma=False
    )
```

```python
import functools
import math

import jax
import jax.numpy as jnp
from jax import lax
from jax.experimental import pallas as pl
from jax.experimental.pallas import tpu as pltpu
from jax.sharding import PartitionSpec as P


HEAD_DIM = 128
STEPS = 2
LAGS = 2
LEVELS = 1000

SIGMA_SHIFT = 5.0
EPSILON = 1e-06
MASKED = -1e30
AXIS = "fsdp"


def sigma_of(levels):
    fraction = levels.astype(jnp.float32) / LEVELS
    return SIGMA_SHIFT * fraction / (1.0 + (SIGMA_SHIFT - 1.0) * fraction)


def frequencies(half_count):
    return jnp.exp(-math.log(10000.0) * jnp.arange(half_count, dtype=jnp.float32) / half_count)


def modulation(sigmas, time_proj):
    half_count = time_proj.shape[0] // 2
    angles = 1000.0 * sigmas[:, None] * frequencies(half_count)[None, :]
    features = jnp.concatenate([jnp.cos(angles), jnp.sin(angles)], axis=1).astype(jnp.bfloat16)
    return jnp.dot(features, time_proj, preferred_element_type=jnp.float32)


def modulate(latent, shift, scale):
    parts = shift.shape[0]
    values = latent.astype(jnp.float32).reshape(parts, -1, latent.shape[1])
    centred = values - jnp.mean(values, axis=-1, keepdims=True)
    variance = jnp.mean(centred * centred, axis=-1, keepdims=True)
    normed = centred * lax.rsqrt(variance + EPSILON)
    result = normed * (1.0 + scale[:, None, :]) + shift[:, None, :]
    return result.astype(jnp.bfloat16).reshape(latent.shape)


def permute(value, target_of):
    pairs = [(s, target_of(s)) for s in range(lax.axis_size(AXIS))]
    return lax.ppermute(value, AXIS, [(s, t) for s, t in pairs if t is not None])


def swap_core(value):
    return permute(value, lambda s: s ^ 1)


def swap_x(value):
    return permute(value, lambda s: s ^ 2)


def swap_y(value):
    return permute(value, lambda s: s ^ 4)


def swap_z_pair(value):
    return permute(value, lambda s: s ^ 8)


def swap_z_middle(value):
    return permute(value, lambda s: {1: s + 8, 2: s - 8}.get(s // 8))


def z_outward(value):
    return permute(value, lambda s: {1: s - 8, 2: s + 8}.get(s // 8))


def across_plane(value):
    half = value.shape[0] // 2
    from_x = swap_x(value)
    from_y = swap_y(value)
    low, high = from_x[:half], from_y[half:]
    return [value, from_x, from_y, swap_y(low), swap_x(high)]


def across_plane_in_halves(value):
    half = value.shape[0] // 2
    low, high = value[:half], value[half:]
    low_x = swap_x(low)
    high_y = swap_y(high)
    high_x = swap_x(high)
    low_y = swap_y(low)
    return [value, low_x, high_x, low_y, high_y, swap_y(low_x), swap_x(high_y)]


def gather_block(unit, device):
    z = device // 8
    place = (device // 2) % 4
    middle = (z == 1) | (z == 2)
    pair = swap_z_pair(unit)
    across = swap_z_middle(unit)
    two_mid = swap_z_middle(pair)
    two_end = z_outward(across)
    second = jnp.where(middle, two_mid, two_end)
    three_end = z_outward(second)
    third = jnp.where(middle, across, three_end)
    slots = [unit, pair, second, third]
    pieces = [across_plane(slot) for slot in slots[:3]]
    pieces.append(across_plane_in_halves(third))
    rows = unit.shape[0]
    halves = [[(i, 0, rows // 2), (i, rows // 2, rows // 2)] for i in range(4)]
    spots = [[(0, 0, rows), (1, 0, rows), (2, 0, rows)] + halves[3]] * 3
    spots.append([(0, 0, rows)] + halves[1] + halves[2] + halves[3])
    return [z ^ step for step in range(4)], place, pieces, spots


def gather_rest(unit, device):
    z = device // 8
    place = (device // 2) % 4
    middle = (z == 1) | (z == 2)
    half = unit.shape[0] // 2
    from_x = swap_x(unit)
    from_y = swap_y(unit)
    low, high = from_x[:half], from_y[half:]
    low, high = swap_y(low), swap_x(high)
    plane = jnp.zeros((4,) + unit.shape, unit.dtype)
    far = jnp.concatenate([low, high], axis=0)
    for piece, at in ((unit, place), (from_x, place ^ 1), (from_y, place ^ 2), (far, place ^ 3)):
        plane = lax.dynamic_update_slice(plane, piece[None], (at, 0, 0))
    plane = plane.reshape(-1, unit.shape[1])
    pair = swap_z_pair(plane)
    across = swap_z_middle(plane)
    two_mid = swap_z_middle(pair)
    two_end = z_outward(across)
    second = jnp.where(middle, two_mid, two_end)
    three_end = z_outward(second)
    return [plane, pair, second, jnp.where(middle, across, three_end)]


def gather_any(unit, device):
    size = lax.axis_size(AXIS)
    groups = [list(range(core, size, 2)) for core in range(2)]
    whole = lax.all_gather(unit, AXIS, axis=0, tiled=True, axis_index_groups=groups)
    none = jnp.int32(0)
    return [none], none, [[whole]], [[(0, 0, whole.shape[0])]]


def gather_rest_any(unit, device):
    return gather_any(unit, device)[2][0]


def absorb_body(spots, step, has_sum, last, places_ref, hidden_ref, *refs):
    count = len(spots)
    piece_refs, refs = refs[:count], refs[count:]
    if has_sum:
        raw_in_ref, past_in_ref, *refs = refs
    if last:
        rest_ref, past_rest_ref, *refs = refs
    plane_out_ref, raw_ref, past_ref, *refs = refs
    if last:
        sum_ref, *refs = refs
    plane_ref, sems, out_sem = refs
    place = places_ref[places_ref.shape[0] - 2]
    copies = []
    for i, (other, start, size) in enumerate(spots):
        target = plane_ref.at[jnp.bitwise_xor(place, other), pl.ds(start, size), :]
        copies.append(pltpu.make_async_copy(piece_refs[i], target, sems.at[i]))
    for copy in copies:
        copy.start()
    for copy in copies:
        copy.wait()
    out = pltpu.make_async_copy(plane_ref, plane_out_ref, out_sem)
    out.start()
    weights = plane_ref[...].reshape(-1, plane_ref.shape[2])
    hidden = hidden_ref[places_ref[step]]
    split = weights.shape[1] // 2
    rows = raw_ref.shape[0]
    raw = jnp.dot(hidden[:rows], weights, preferred_element_type=jnp.float32)
    past = jnp.dot(hidden[rows:], weights[:, split:], preferred_element_type=jnp.float32)
    if has_sum:
        raw = raw + raw_in_ref[...]
        past = past + past_in_ref[...]
    if not last:
        raw_ref[...] = raw
        past_ref[...] = past
    else:
        rest, past_rest = rest_ref[...], past_rest_ref[...]
        more = past_rest.shape[1]
        half = split + more
        at = 0
        for target, start, main, other in (
            (raw_ref, 0, raw[:, :split], rest[:, :more]),
            (raw_ref, half, raw[:, split:], rest[:, more:]),
            (past_ref, 0, past, past_rest),
        ):
            target[:, start : start + split] = main
            target[:, start + split : start + half] = other
            count = main.shape[0]
            total = jnp.sum(main * main, -1, keepdims=True)
            total = total + jnp.sum(other * other, -1, keepdims=True)
            sum_ref[at : at + count] = jnp.broadcast_to(total, (count, HEAD_DIM))
            at += count
    out.wait()


def absorb(step, places, hidden, pieces, spots, chips, rows, sums, rests):
    last = bool(rests)
    hbm = pl.BlockSpec(memory_space=pltpu.HBM)
    vmem = pl.BlockSpec(memory_space=pltpu.VMEM)
    width = pieces[0].shape[1]
    chip_rows = hidden.shape[2] // chips
    past_rows = hidden.shape[1] - rows
    more = rests[1].shape[1] if last else 0
    operands = [places, hidden, *pieces, *sums, *rests]
    specs = [pl.BlockSpec(memory_space=pltpu.SMEM), vmem] + [hbm] * len(pieces)
    specs += [vmem] * (len(sums) + len(rests))
    shapes = [
        pltpu.HBM((chips, chip_rows, width), jnp.bfloat16),
        jax.ShapeDtypeStruct((rows, width + 2 * more), jnp.float32),
        jax.ShapeDtypeStruct((past_rows, width // 2 + more), jnp.float32),
    ]
    outs = [hbm, vmem, vmem]
    if last:
        shapes.append(jax.ShapeDtypeStruct((2 * rows + past_rows, HEAD_DIM), jnp.float32))
        outs.append(vmem)
    return pl.pallas_call(
        functools.partial(absorb_body, spots, step, bool(sums), last),
        in_specs=specs,
        out_specs=outs,
        out_shape=shapes,
        scratch_shapes=[
            pltpu.VMEM((chips, chip_rows, width), jnp.bfloat16),
            pltpu.SemaphoreType.DMA((len(pieces),)),
            pltpu.SemaphoreType.DMA,
        ],
        compiler_params=pltpu.CompilerParams(vmem_limit_bytes=16 << 20),
        name="absorb",
    )(*operands)


def absorb_rest_body(places_ref, hidden_ref, *refs):
    count = len(refs) - 4
    plane_refs = refs[:count]
    raw_ref, past_ref, weight_ref, sems = refs[count:]
    copies = [
        pltpu.make_async_copy(ref, weight_ref.at[i], sems.at[i]) for i, ref in enumerate(plane_refs)
    ]
    for copy in copies:
        copy.start()
    rows, split = raw_ref.shape[0], past_ref.shape[1]
    raw = past = None
    for i, copy in enumerate(copies):
        copy.wait()
        hidden, weights = hidden_ref[places_ref[i]], weight_ref[i]
        part = jnp.dot(hidden[:rows], weights, preferred_element_type=jnp.float32)
        raw = part if raw is None else raw + part
        part = jnp.dot(hidden[rows:], weights[:, split:], preferred_element_type=jnp.float32)
        past = part if past is None else past + part
    raw_ref[...] = raw
    past_ref[...] = past


def absorb_rest(places, hidden, planes, rows):
    hbm = pl.BlockSpec(memory_space=pltpu.HBM)
    vmem = pl.BlockSpec(memory_space=pltpu.VMEM)
    count, width = len(planes), planes[0].shape[1]
    return pl.pallas_call(
        absorb_rest_body,
        in_specs=[pl.BlockSpec(memory_space=pltpu.SMEM), vmem] + [hbm] * count,
        out_shape=[
            jax.ShapeDtypeStruct((rows, width), jnp.float32),
            jax.ShapeDtypeStruct((hidden.shape[1] - rows, width // 2), jnp.float32),
        ],
        scratch_shapes=[
            pltpu.VMEM((count,) + planes[0].shape, jnp.bfloat16),
            pltpu.SemaphoreType.DMA((count,)),
        ],
        compiler_params=pltpu.CompilerParams(vmem_limit_bytes=12 << 20),
        name="absorb_rest",
    )(places, hidden, *planes)


def turn(values, cosine, sine):
    return values * cosine + pltpu.roll(values, HEAD_DIM // 2, 1) * sine


def attend_body(first, inner, *refs):
    (raw_ref, own_sum_ref, other_sum_ref, q_gain_ref, k_gain_ref, cos_ref, sin_ref,
     usable_ref, v_ref, past_v_ref, latent_ref, factor_ref, *refs) = refs
    if first:
        past_ref, out_ref, past_key_ref = refs
    else:
        past_key_ref, out_ref = refs
    rows, width = latent_ref.shape
    extra = past_v_ref.shape[0]
    heads = width // HEAD_DIM
    scale = lax.rsqrt((own_sum_ref[...] + other_sum_ref[...]) / inner + EPSILON)
    q_scale, k_scale = scale[:rows], scale[rows : 2 * rows]
    turned = slice(extra - rows // 2, extra + rows // 2)
    own_cos, own_sin = cos_ref[turned, :], sin_ref[turned, :]

    def per_row(pair):
        rows_of = [jnp.broadcast_to(pair[i : i + 1], (rows // 2, pair.shape[1])) for i in range(2)]
        return jnp.concatenate(rows_of, axis=0)

    allowed = per_row(usable_ref[...]) > 0.0
    for head in range(heads):
        at = slice(head * HEAD_DIM, (head + 1) * HEAD_DIM)
        key_at = slice(width + at.start, width + at.stop)
        query = raw_ref[:, at] * q_scale * q_gain_ref[:, at]
        query = turn(query, own_cos, own_sin).astype(jnp.bfloat16)
        key = raw_ref[:, key_at] * k_scale * k_gain_ref[:, at]
        key = turn(key, own_cos, own_sin).astype(jnp.bfloat16)
        if first:
            past = past_ref[:, at] * scale[2 * rows :] * k_gain_ref[:, at]
            past = turn(past, cos_ref[:extra, :], sin_ref[:extra, :]).astype(jnp.bfloat16)
            past_key_ref[:, at] = past
        else:
            past = past_key_ref[:, at]
        keys = jnp.concatenate([key, past], axis=0)
        values = jnp.concatenate([v_ref[:, at], past_v_ref[:, at]], axis=0)
        scores = lax.dot_general(
            query, keys, (((1,), (1,)), ((), ())), preferred_element_type=jnp.float32
        ) * HEAD_DIM ** (-0.5)
        scores = jnp.where(allowed, scores, MASKED)
        expanded = jnp.exp(scores - jnp.max(scores, axis=-1, keepdims=True))
        weights = (expanded / jnp.sum(expanded, axis=-1, keepdims=True)).astype(jnp.bfloat16)
        mixed = jnp.dot(weights, values, preferred_element_type=jnp.float32).astype(jnp.bfloat16)
        step = per_row(factor_ref[:, at]) * mixed.astype(jnp.float32)
        out_ref[:, at] = (latent_ref[:, at].astype(jnp.float32) + step).astype(jnp.bfloat16)


def attend(first, inner, raw, sums, others, gains, tables, fixed, latent, factor, past):
    shapes = [jax.ShapeDtypeStruct(latent.shape, jnp.bfloat16)]
    if first:
        shapes.append(pltpu.HBM(past.shape, jnp.bfloat16))
    else:
        own_values, past_values = fixed[1:]
        raw, past, own_values, sums, others = (
            pltpu.with_memory_space_constraint(x, pltpu.HBM)
            for x in (raw, past, own_values, sums, others)
        )
        fixed = (fixed[0], own_values, past_values)
    return pl.pallas_call(
        functools.partial(attend_body, first, inner),
        out_shape=shapes,
        compiler_params=pltpu.CompilerParams(vmem_limit_bytes=16 << 20),
        name="attend",
    )(raw, sums, others, *gains, *tables, *fixed, latent, factor, past)


def project_body(places_ref, own_ref, other_ref, mod_ref, *refs):
    count = (len(refs) - 7) // 2
    raw_ref, sum_ref, value_ref, hidden_ref, main_ref, rest_ref, sems = refs[2 * count :]
    targets = [main_ref.at[i] for i in range(count)] + [rest_ref.at[i] for i in range(count)]
    rows, half = own_ref.shape
    parts, _, part_width = hidden_ref.shape
    copies = [
        pltpu.make_async_copy(ref, target, sems.at[i])
        for i, (ref, target) in enumerate(zip(refs, targets))
    ]
    for copy in copies:
        copy.start()
    is_low = places_ref[count + 1] == 0
    own, other = own_ref[...].astype(jnp.float32), other_ref[...].astype(jnp.float32)
    low, high = jnp.where(is_low, own, other), jnp.where(is_low, other, own)
    width = 2 * half
    mean = (jnp.sum(low, -1, keepdims=True) + jnp.sum(high, -1, keepdims=True)) / width
    low, high = low - mean, high - mean
    variance = (
        jnp.sum(low * low, -1, keepdims=True) + jnp.sum(high * high, -1, keepdims=True)
    ) / width
    scale = lax.rsqrt(variance + EPSILON)
    sides = []
    for side, centred in enumerate((low, high)):
        normed = centred * scale
        at = slice(side * half, (side + 1) * half)
        gain_at = slice(width + side * half, width + (side + 1) * half)
        pieces = []
        for span in range(2):
            piece = normed[span * (rows // 2) : (span + 1) * (rows // 2)]
            row = slice(3 + span, 4 + span)
            pieces.append(piece * (1.0 + mod_ref[row, gain_at]) + mod_ref[row, at])
        sides.append(jnp.concatenate(pieces, axis=0).astype(jnp.bfloat16))
    value_ref[...] = jnp.where(is_low, sides[0], sides[1])
    for i in range(parts):
        for side in range(2):
            if parts == 1:
                hidden_ref[0, :, side * half : (side + 1) * half] = sides[side]
            elif i * part_width // half == side:
                at = i * part_width - side * half
                hidden_ref[i] = sides[side][:, at : at + part_width]
    squares = [None, None]
    start = 0
    for weight_ref, waits in ((main_ref, copies[:count]), (rest_ref, copies[count:])):
        total = None
        for i, copy in enumerate(waits):
            copy.wait()
            weights = weight_ref[i].reshape(-1, weight_ref.shape[-1])
            part = jnp.dot(hidden_ref[places_ref[i]], weights, preferred_element_type=jnp.float32)
            total = part if total is None else total + part
        split = total.shape[1] // 2
        for i in range(2):
            side = total[:, i * split : (i + 1) * split]
            raw_ref[:, i * half + start : i * half + start + split] = side
            square = jnp.sum(side * side, -1, keepdims=True)
            squares[i] = square if squares[i] is None else squares[i] + square
        start += split
    for i in range(2):
        sum_ref[i * rows : (i + 1) * rows] = jnp.broadcast_to(squares[i], (rows, HEAD_DIM))


def project_latent(places, own, other, mods, planes, rests):
    rows, half = own.shape
    count = len(planes)
    planes, rests = (
        [pltpu.with_memory_space_constraint(plane, pltpu.HBM) for plane in group]
        for group in (planes, rests)
    )
    vmem = pl.BlockSpec(memory_space=pltpu.VMEM)
    hbm = pl.BlockSpec(memory_space=pltpu.HBM)
    return pl.pallas_call(
        project_body,
        in_specs=[pl.BlockSpec(memory_space=pltpu.SMEM)] + [vmem] * 3 + [hbm] * (2 * count),
        out_shape=[
            pltpu.HBM((rows, 2 * half), jnp.float32),
            pltpu.HBM((2 * rows, HEAD_DIM), jnp.float32),
            pltpu.HBM((rows, half), jnp.bfloat16),
        ],
        scratch_shapes=[
            pltpu.VMEM((count, rows, 2 * half // count), jnp.bfloat16),
            pltpu.VMEM((count,) + planes[0].shape, jnp.bfloat16),
            pltpu.VMEM((count,) + rests[0].shape, jnp.bfloat16),
            pltpu.SemaphoreType.DMA((2 * count,)),
        ],
        compiler_params=pltpu.CompilerParams(vmem_limit_bytes=24 << 20),
        name="project",
    )(places, own, other, mods, *planes, *rests)


def denoise(noisy, clean, seg_ids, lag_mask, plan, w_query, w_key, time_proj, q_gain, k_gain):
    rows, width = noisy.shape
    inner = w_query.shape[1]
    half = inner // 2
    devices = lax.axis_size(AXIS)
    device = lax.axis_index(AXIS)
    core = device % 2
    first_span = device - core
    is_low = core == 0

    def mine(value, axis):
        return lax.dynamic_slice_in_dim(value, core * half, half, axis)

    def in_order(own, other, axis):
        low = jnp.where(is_low, own, other)
        high = jnp.where(is_low, other, own)
        return jnp.concatenate([low, high], axis=axis)

    before = permute(clean, lambda s: s + 2 if s + 2 < devices else None)
    others = swap_core(clean)

    split = (half // HEAD_DIM) * 4 // 5 * HEAD_DIM

    def columns(start, low, high):
        return jnp.concatenate(
            [lax.dynamic_slice_in_dim(w, start + low, high - low, 1) for w in (w_query, w_key)],
            axis=1,
        )

    own_start, other_start = core * half, (1 - core) * half
    unit = in_order(
        columns(own_start, 0, split), swap_core(columns(other_start, 0, split)), 0
    )
    sent_rest = swap_core(columns(other_start, split, half))
    rest_unit = in_order(columns(own_start, split, half), sent_rest, 0)
    unit, noisy, seg_ids, plan, lag_mask, time_proj = lax.optimization_barrier(
        (unit, noisy, seg_ids, plan, lag_mask, time_proj)
    )
    on_block = devices == 32
    plane_ids, place, pieces, spots = (gather_block if on_block else gather_any)(unit, device)
    rests = (gather_rest if on_block else gather_rest_any)(rest_unit, device)
    noisy_both = in_order(noisy, swap_core(noisy), 0)
    small = jnp.concatenate([plan, lag_mask], axis=1)
    small_both = in_order(small, swap_core(small), 0)
    plan_both, lags_both = small_both[:, :STEPS], small_both[:, STEPS:]
    sigmas = [sigma_of(plan_both[:, j]) for j in range(STEPS)] + [jnp.zeros((2,), jnp.float32)]
    mods = modulation(jnp.concatenate([jnp.zeros((1,), jnp.float32)] + sigmas[:STEPS]), time_proj)
    step_mods = [mods[1 + 2 * j : 3 + 2 * j] for j in range(STEPS)]
    hidden = modulate(noisy_both, step_mods[0][:, :width], step_mods[0][:, width : 2 * width])
    latent = mine(noisy_both, 1)
    values = mine(hidden, 1)

    before_both = in_order(before, swap_core(before), 0)
    past_clean = jnp.concatenate([before_both, jnp.where(is_low, clean, others)], axis=0)
    past_hidden = modulate(past_clean, mods[:1, :width], mods[:1, width : 2 * width])
    past_values = mine(past_hidden, 1)
    stack = jnp.concatenate([hidden, past_hidden], axis=0)
    stack = stack.reshape(stack.shape[0], len(plane_ids), -1).swapaxes(0, 1)
    places = jnp.stack(plane_ids + [place, core]).astype(jnp.int32)

    factors = [
        (sigmas[j + 1] - sigmas[j])[:, None] * mine(step_mods[j][:, 2 * width :], 1)
        for j in range(STEPS)
    ]
    gains = (mine(q_gain, 0)[None, :], mine(k_gain, 0)[None, :])
    spans = jnp.maximum(first_span - 2 + jnp.arange(4, dtype=jnp.int32), 0)
    segments = seg_ids[spans]
    starts = jnp.sum((seg_ids[None, :] < segments[:, None]).astype(jnp.int32), axis=1)
    positions = (
        (spans - starts)[:, None] * rows + jnp.arange(rows, dtype=jnp.int32)[None, :]
    ).astype(jnp.float32).reshape(-1, 1)
    angles = positions * frequencies(HEAD_DIM // 2)[None, :]
    cosine = jnp.concatenate([jnp.cos(angles)] * 2, axis=1)
    sine = jnp.concatenate([-jnp.sin(angles), jnp.sin(angles)], axis=1)
    tables = (cosine, sine)
    block = jnp.arange(5 * rows, dtype=jnp.int32)[None, :] // rows
    here = jnp.arange(2, dtype=jnp.int32)[:, None]
    usable = block == here
    for lag in range(1, LAGS + 1):
        allowed = (
            (first_span + here >= lag)
            & (segments[2 - lag : 4 - lag] == segments[2:])[:, None]
            & (lags_both[:, lag - 1 : lag] == 1)
        )
        usable = usable | (allowed & (block == here + 4 - lag))
    usable = usable.astype(jnp.float32)

    chips = 4 if len(pieces) == 4 else 1
    more = absorb_rest(places, stack, rests, 2 * rows)
    sums, planes = [], []
    for step, parts in enumerate(pieces):
        final = more if step + 1 == len(pieces) else []
        plane, *sums = absorb(step, places, stack, parts, spots[step], chips, 2 * rows, sums, final)
        planes.append(plane)
    raw, past_raw, sums = sums
    latent, past_key = attend(
        True, inner, raw, sums, swap_core(sums), gains, tables, (usable, values, past_values),
        latent, factors[0], past_raw,
    )
    raw, sums, values = project_latent(places, latent, swap_core(latent), mods, planes, rests)
    (latent,) = attend(
        False, inner, raw, sums, swap_core(sums), gains, tables, (usable, values, past_values),
        latent, factors[1], past_key,
    )
    kept = lax.dynamic_slice_in_dim(latent, core * rows, rows, 0)
    sent = lax.dynamic_slice_in_dim(latent, (1 - core) * rows, rows, 0)
    return in_order(kept, swap_core(sent), 1)


def solution(mesh):
    placed = (
        P(("pool", "fsdp"), None),
        P(("pool", "fsdp"), None),
        P("pool"),
        P(("pool", "fsdp"), None),
        P(("pool", "fsdp"), None),
        P("fsdp", None),
        P("fsdp", None),
        P(),
        P(),
        P(),
    )
    return jax.shard_map(
        denoise, mesh=mesh, in_specs=placed, out_specs=P(("pool", "fsdp"), None), check_vma=False
    )
```

```python
import functools
import math

import jax
import jax.numpy as jnp
from jax import lax
from jax.experimental import pallas as pl
from jax.experimental.pallas import tpu as pltpu
from jax.sharding import PartitionSpec as P


HEAD_DIM = 128
STEPS = 2
LAGS = 2
LEVELS = 1000

SIGMA_SHIFT = 5.0
EPSILON = 1e-06
MASKED = -1e30
AXIS = "fsdp"


def sigma_of(levels):
    fraction = levels.astype(jnp.float32) / LEVELS
    return SIGMA_SHIFT * fraction / (1.0 + (SIGMA_SHIFT - 1.0) * fraction)


def frequencies(half_count):
    return jnp.exp(-math.log(10000.0) * jnp.arange(half_count, dtype=jnp.float32) / half_count)


def modulation(sigmas, time_proj):
    half_count = time_proj.shape[0] // 2
    angles = 1000.0 * sigmas[:, None] * frequencies(half_count)[None, :]
    features = jnp.concatenate([jnp.cos(angles), jnp.sin(angles)], axis=1).astype(jnp.bfloat16)
    return jnp.dot(features, time_proj, preferred_element_type=jnp.float32)


def modulate(latent, shift, scale):
    parts = shift.shape[0]
    values = latent.astype(jnp.float32).reshape(parts, -1, latent.shape[1])
    centred = values - jnp.mean(values, axis=-1, keepdims=True)
    variance = jnp.mean(centred * centred, axis=-1, keepdims=True)
    normed = centred * lax.rsqrt(variance + EPSILON)
    result = normed * (1.0 + scale[:, None, :]) + shift[:, None, :]
    return result.astype(jnp.bfloat16).reshape(latent.shape)


def permute(value, target_of):
    pairs = [(s, target_of(s)) for s in range(lax.axis_size(AXIS))]
    return lax.ppermute(value, AXIS, [(s, t) for s, t in pairs if t is not None])


def swap_core(value):
    return permute(value, lambda s: s ^ 1)


def swap_x(value):
    return permute(value, lambda s: s ^ 2)


def swap_y(value):
    return permute(value, lambda s: s ^ 4)


def swap_z_pair(value):
    return permute(value, lambda s: s ^ 8)


def swap_z_middle(value):
    return permute(value, lambda s: {1: s + 8, 2: s - 8}.get(s // 8))


def z_outward(value):
    return permute(value, lambda s: {1: s - 8, 2: s + 8}.get(s // 8))


def across_plane(value):
    half = value.shape[0] // 2
    from_x = swap_x(value)
    from_y = swap_y(value)
    low, high = from_x[:half], from_y[half:]
    return [value, from_x, from_y, swap_y(low), swap_x(high)]


def across_plane_in_halves(value):
    half = value.shape[0] // 2
    low, high = value[:half], value[half:]
    low_x = swap_x(low)
    high_y = swap_y(high)
    high_x = swap_x(high)
    low_y = swap_y(low)
    return [value, low_x, high_x, low_y, high_y, swap_y(low_x), swap_x(high_y)]


def gather_block(unit, device):
    z = device // 8
    place = (device // 2) % 4
    middle = (z == 1) | (z == 2)
    pair = swap_z_pair(unit)
    across = swap_z_middle(unit)
    two_mid = swap_z_middle(pair)
    two_end = z_outward(across)
    second = jnp.where(middle, two_mid, two_end)
    three_end = z_outward(second)
    third = jnp.where(middle, across, three_end)
    slots = [unit, pair, second, third]
    pieces = [across_plane(slot) for slot in slots[:3]]
    pieces.append(across_plane_in_halves(third))
    rows = unit.shape[0]
    halves = [[(i, 0, rows // 2), (i, rows // 2, rows // 2)] for i in range(4)]
    spots = [[(0, 0, rows), (1, 0, rows), (2, 0, rows)] + halves[3]] * 3
    spots.append([(0, 0, rows)] + halves[1] + halves[2] + halves[3])
    return [z ^ step for step in range(4)], place, pieces, spots


def gather_rest(unit, device):
    z = device // 8
    place = (device // 2) % 4
    middle = (z == 1) | (z == 2)
    half = unit.shape[0] // 2
    from_x = swap_x(unit)
    from_y = swap_y(unit)
    low, high = from_x[:half], from_y[half:]
    low, high = swap_y(low), swap_x(high)
    plane = jnp.zeros((4,) + unit.shape, unit.dtype)
    far = jnp.concatenate([low, high], axis=0)
    for piece, at in ((unit, place), (from_x, place ^ 1), (from_y, place ^ 2), (far, place ^ 3)):
        plane = lax.dynamic_update_slice(plane, piece[None], (at, 0, 0))
    plane = plane.reshape(-1, unit.shape[1])
    pair = swap_z_pair(plane)
    across = swap_z_middle(plane)
    two_mid = swap_z_middle(pair)
    two_end = z_outward(across)
    second = jnp.where(middle, two_mid, two_end)
    three_end = z_outward(second)
    return [plane, pair, second, jnp.where(middle, across, three_end)]


def gather_any(unit, device):
    size = lax.axis_size(AXIS)
    groups = [list(range(core, size, 2)) for core in range(2)]
    whole = lax.all_gather(unit, AXIS, axis=0, tiled=True, axis_index_groups=groups)
    none = jnp.int32(0)
    return [none], none, [[whole]], [[(0, 0, whole.shape[0])]]


def gather_rest_any(unit, device):
    return gather_any(unit, device)[2][0]


def absorb_body(spots, step, has_sum, rest_count, places_ref, hidden_ref, *refs):
    count = len(spots)
    piece_refs, refs = refs[:count], refs[count:]
    if has_sum:
        raw_in_ref, past_in_ref, *refs = refs
    rest_refs, refs = refs[:rest_count], refs[rest_count:]
    plane_out_ref, raw_ref, past_ref, *refs = refs
    if rest_count:
        sum_ref, plane_ref, sems, out_sem, rest_ref, rest_sems = refs
    else:
        plane_ref, sems, out_sem = refs
    place = places_ref[places_ref.shape[0] - 2]
    copies = []
    for i, (other, start, size) in enumerate(spots):
        target = plane_ref.at[jnp.bitwise_xor(place, other), pl.ds(start, size), :]
        copies.append(pltpu.make_async_copy(piece_refs[i], target, sems.at[i]))
    rest_copies = [
        pltpu.make_async_copy(ref, rest_ref.at[i], rest_sems.at[i])
        for i, ref in enumerate(rest_refs)
    ]
    for copy in copies + rest_copies:
        copy.start()
    rows = raw_ref.shape[0]

    def multiply(index, weights):
        split = weights.shape[1] // 2
        hidden = hidden_ref[places_ref[index]]
        query = jnp.dot(hidden[:rows], weights[:, :split], preferred_element_type=jnp.float32)
        keys = jnp.dot(hidden, weights[:, split:], preferred_element_type=jnp.float32)
        return query, keys[:rows], keys[rows:]

    for copy in copies:
        copy.wait()
    out = pltpu.make_async_copy(plane_ref, plane_out_ref, out_sem)
    out.start()
    main = multiply(step, plane_ref[...].reshape(-1, plane_ref.shape[2]))
    split = main[0].shape[1]
    if has_sum:
        before = raw_in_ref[:, :split], raw_in_ref[:, split:], past_in_ref[...]
        main = [part + other for part, other in zip(main, before)]
    if rest_count:
        rest = None
        for i, copy in enumerate(rest_copies):
            copy.wait()
            parts = multiply(i, rest_ref[i])
            rest = parts if rest is None else [x + y for x, y in zip(rest, parts)]
        more = rest[0].shape[1]
    else:
        rest, more = [None] * 3, 0
    at = 0
    targets = (raw_ref, 0), (raw_ref, split + more), (past_ref, 0)
    for (target, start), part, other in zip(targets, main, rest):
        target[:, start : start + split] = part
        if rest_count:
            target[:, start + split : start + split + more] = other
            total = jnp.sum(part * part, -1, keepdims=True)
            total = total + jnp.sum(other * other, -1, keepdims=True)
            size = total.shape[0]
            sum_ref[at : at + size] = jnp.broadcast_to(total, (size, HEAD_DIM))
            at += size
    out.wait()


def absorb(step, places, hidden, pieces, spots, chips, rows, sums, rests):
    hbm = pl.BlockSpec(memory_space=pltpu.HBM)
    vmem = pl.BlockSpec(memory_space=pltpu.VMEM)
    width = pieces[0].shape[1]
    more = rests[0].shape[1] if rests else 0
    chip_rows = hidden.shape[2] // chips
    past_rows = hidden.shape[1] - rows
    operands = [places, hidden, *pieces, *sums, *rests]
    specs = [pl.BlockSpec(memory_space=pltpu.SMEM), vmem] + [hbm] * len(pieces)
    specs += [vmem] * len(sums) + [hbm] * len(rests)
    shapes = [
        pltpu.HBM((chips, chip_rows, width), jnp.bfloat16),
        jax.ShapeDtypeStruct((rows, width + more), jnp.float32),
        jax.ShapeDtypeStruct((past_rows, (width + more) // 2), jnp.float32),
    ]
    outs = [hbm, vmem, vmem]
    scratch = [
        pltpu.VMEM((chips, chip_rows, width), jnp.bfloat16),
        pltpu.SemaphoreType.DMA((len(pieces),)),
        pltpu.SemaphoreType.DMA,
    ]
    if rests:
        shapes.append(jax.ShapeDtypeStruct((2 * rows + past_rows, HEAD_DIM), jnp.float32))
        outs.append(vmem)
        scratch.append(pltpu.VMEM((len(rests),) + rests[0].shape, jnp.bfloat16))
        scratch.append(pltpu.SemaphoreType.DMA((len(rests),)))
    return pl.pallas_call(
        functools.partial(absorb_body, spots, step, bool(sums), len(rests)),
        in_specs=specs,
        out_specs=outs,
        out_shape=shapes,
        scratch_shapes=scratch,
        compiler_params=pltpu.CompilerParams(vmem_limit_bytes=16 << 20),
        name="absorb",
    )(*operands)


def turn(values, cosine, sine):
    return values * cosine + pltpu.roll(values, HEAD_DIM // 2, 1) * sine


def attend_body(first, inner, *refs):
    (raw_ref, own_sum_ref, other_sum_ref, q_gain_ref, k_gain_ref, cos_ref, sin_ref,
     usable_ref, v_ref, past_v_ref, latent_ref, factor_ref, *refs) = refs
    if first:
        past_ref, out_ref, past_key_ref = refs
    else:
        past_key_ref, out_ref = refs
    rows, width = latent_ref.shape
    extra = past_v_ref.shape[0]
    heads = width // HEAD_DIM
    scale = lax.rsqrt((own_sum_ref[...] + other_sum_ref[...]) / inner + EPSILON)
    q_scale, k_scale = scale[:rows], scale[rows : 2 * rows]
    turned = slice(extra - rows // 2, extra + rows // 2)
    own_cos, own_sin = cos_ref[turned, :], sin_ref[turned, :]

    def per_row(pair):
        rows_of = [jnp.broadcast_to(pair[i : i + 1], (rows // 2, pair.shape[1])) for i in range(2)]
        return jnp.concatenate(rows_of, axis=0)

    allowed = per_row(usable_ref[...]) > 0.0
    for head in range(heads):
        at = slice(head * HEAD_DIM, (head + 1) * HEAD_DIM)
        key_at = slice(width + at.start, width + at.stop)
        query = raw_ref[:, at] * q_scale * q_gain_ref[:, at]
        query = turn(query, own_cos, own_sin).astype(jnp.bfloat16)
        key = raw_ref[:, key_at] * k_scale * k_gain_ref[:, at]
        key = turn(key, own_cos, own_sin).astype(jnp.bfloat16)
        if first:
            past = past_ref[:, at] * scale[2 * rows :] * k_gain_ref[:, at]
            past = turn(past, cos_ref[:extra, :], sin_ref[:extra, :]).astype(jnp.bfloat16)
            past_key_ref[:, at] = past
        else:
            past = past_key_ref[:, at]
        keys = jnp.concatenate([key, past], axis=0)
        values = jnp.concatenate([v_ref[:, at], past_v_ref[:, at]], axis=0)
        scores = lax.dot_general(
            query, keys, (((1,), (1,)), ((), ())), preferred_element_type=jnp.float32
        ) * HEAD_DIM ** (-0.5)
        scores = jnp.where(allowed, scores, MASKED)
        expanded = jnp.exp(scores - jnp.max(scores, axis=-1, keepdims=True))
        weights = (expanded / jnp.sum(expanded, axis=-1, keepdims=True)).astype(jnp.bfloat16)
        mixed = jnp.dot(weights, values, preferred_element_type=jnp.float32).astype(jnp.bfloat16)
        step = per_row(factor_ref[:, at]) * mixed.astype(jnp.float32)
        out_ref[:, at] = (latent_ref[:, at].astype(jnp.float32) + step).astype(jnp.bfloat16)


def attend(first, inner, raw, sums, others, gains, tables, fixed, latent, factor, past):
    shapes = [jax.ShapeDtypeStruct(latent.shape, jnp.bfloat16)]
    if first:
        shapes.append(pltpu.HBM(past.shape, jnp.bfloat16))
    else:
        own_values, past_values = fixed[1:]
        raw, past, own_values, sums, others = (
            pltpu.with_memory_space_constraint(x, pltpu.HBM)
            for x in (raw, past, own_values, sums, others)
        )
        fixed = (fixed[0], own_values, past_values)
    return pl.pallas_call(
        functools.partial(attend_body, first, inner),
        out_shape=shapes,
        compiler_params=pltpu.CompilerParams(vmem_limit_bytes=16 << 20),
        name="attend",
    )(raw, sums, others, *gains, *tables, *fixed, latent, factor, past)


def project_body(places_ref, own_ref, other_ref, mod_ref, *refs):
    count = (len(refs) - 7) // 2
    raw_ref, sum_ref, value_ref, hidden_ref, main_ref, rest_ref, sems = refs[2 * count :]
    targets = [main_ref.at[i] for i in range(count)] + [rest_ref.at[i] for i in range(count)]
    rows, half = own_ref.shape
    parts, _, part_width = hidden_ref.shape
    copies = [
        pltpu.make_async_copy(ref, target, sems.at[i])
        for i, (ref, target) in enumerate(zip(refs, targets))
    ]
    for copy in copies:
        copy.start()
    is_low = places_ref[count + 1] == 0
    own, other = own_ref[...].astype(jnp.float32), other_ref[...].astype(jnp.float32)
    low, high = jnp.where(is_low, own, other), jnp.where(is_low, other, own)
    width = 2 * half
    mean = (jnp.sum(low, -1, keepdims=True) + jnp.sum(high, -1, keepdims=True)) / width
    low, high = low - mean, high - mean
    variance = (
        jnp.sum(low * low, -1, keepdims=True) + jnp.sum(high * high, -1, keepdims=True)
    ) / width
    scale = lax.rsqrt(variance + EPSILON)
    sides = []
    for side, centred in enumerate((low, high)):
        normed = centred * scale
        at = slice(side * half, (side + 1) * half)
        gain_at = slice(width + side * half, width + (side + 1) * half)
        pieces = []
        for span in range(2):
            piece = normed[span * (rows // 2) : (span + 1) * (rows // 2)]
            row = slice(3 + span, 4 + span)
            pieces.append(piece * (1.0 + mod_ref[row, gain_at]) + mod_ref[row, at])
        sides.append(jnp.concatenate(pieces, axis=0).astype(jnp.bfloat16))
    value_ref[...] = jnp.where(is_low, sides[0], sides[1])
    for i in range(parts):
        for side in range(2):
            if parts == 1:
                hidden_ref[0, :, side * half : (side + 1) * half] = sides[side]
            elif i * part_width // half == side:
                at = i * part_width - side * half
                hidden_ref[i] = sides[side][:, at : at + part_width]
    squares = [None, None]
    start = 0
    for weight_ref, waits in ((main_ref, copies[:count]), (rest_ref, copies[count:])):
        total = None
        for i, copy in enumerate(waits):
            copy.wait()
            weights = weight_ref[i].reshape(-1, weight_ref.shape[-1])
            part = jnp.dot(hidden_ref[places_ref[i]], weights, preferred_element_type=jnp.float32)
            total = part if total is None else total + part
        split = total.shape[1] // 2
        for i in range(2):
            side = total[:, i * split : (i + 1) * split]
            raw_ref[:, i * half + start : i * half + start + split] = side
            square = jnp.sum(side * side, -1, keepdims=True)
            squares[i] = square if squares[i] is None else squares[i] + square
        start += split
    for i in range(2):
        sum_ref[i * rows : (i + 1) * rows] = jnp.broadcast_to(squares[i], (rows, HEAD_DIM))


def project_latent(places, own, other, mods, planes, rests):
    rows, half = own.shape
    count = len(planes)
    planes, rests = (
        [pltpu.with_memory_space_constraint(plane, pltpu.HBM) for plane in group]
        for group in (planes, rests)
    )
    vmem = pl.BlockSpec(memory_space=pltpu.VMEM)
    hbm = pl.BlockSpec(memory_space=pltpu.HBM)
    return pl.pallas_call(
        project_body,
        in_specs=[pl.BlockSpec(memory_space=pltpu.SMEM)] + [vmem] * 3 + [hbm] * (2 * count),
        out_shape=[
            pltpu.HBM((rows, 2 * half), jnp.float32),
            pltpu.HBM((2 * rows, HEAD_DIM), jnp.float32),
            pltpu.HBM((rows, half), jnp.bfloat16),
        ],
        scratch_shapes=[
            pltpu.VMEM((count, rows, 2 * half // count), jnp.bfloat16),
            pltpu.VMEM((count,) + planes[0].shape, jnp.bfloat16),
            pltpu.VMEM((count,) + rests[0].shape, jnp.bfloat16),
            pltpu.SemaphoreType.DMA((2 * count,)),
        ],
        compiler_params=pltpu.CompilerParams(vmem_limit_bytes=24 << 20),
        name="project",
    )(places, own, other, mods, *planes, *rests)


def denoise(noisy, clean, seg_ids, lag_mask, plan, w_query, w_key, time_proj, q_gain, k_gain):
    rows, width = noisy.shape
    inner = w_query.shape[1]
    half = inner // 2
    devices = lax.axis_size(AXIS)
    device = lax.axis_index(AXIS)
    core = device % 2
    first_span = device - core
    is_low = core == 0

    def mine(value, axis):
        return lax.dynamic_slice_in_dim(value, core * half, half, axis)

    def in_order(own, other, axis):
        low = jnp.where(is_low, own, other)
        high = jnp.where(is_low, other, own)
        return jnp.concatenate([low, high], axis=axis)

    before = permute(clean, lambda s: s + 2 if s + 2 < devices else None)
    others = swap_core(clean)

    split = (half // HEAD_DIM) * 4 // 5 * HEAD_DIM

    def columns(start, low, high):
        return jnp.concatenate(
            [lax.dynamic_slice_in_dim(w, start + low, high - low, 1) for w in (w_query, w_key)],
            axis=1,
        )

    own_start, other_start = core * half, (1 - core) * half
    unit = in_order(
        columns(own_start, 0, split), swap_core(columns(other_start, 0, split)), 0
    )
    sent_rest = swap_core(columns(other_start, split, half))
    rest_unit = in_order(columns(own_start, split, half), sent_rest, 0)
    unit, noisy, seg_ids, plan, lag_mask, time_proj = lax.optimization_barrier(
        (unit, noisy, seg_ids, plan, lag_mask, time_proj)
    )
    on_block = devices == 32
    plane_ids, place, pieces, spots = (gather_block if on_block else gather_any)(unit, device)
    rests = (gather_rest if on_block else gather_rest_any)(rest_unit, device)
    noisy_both = in_order(noisy, swap_core(noisy), 0)
    small = jnp.concatenate([plan, lag_mask], axis=1)
    small_both = in_order(small, swap_core(small), 0)
    plan_both, lags_both = small_both[:, :STEPS], small_both[:, STEPS:]
    sigmas = [sigma_of(plan_both[:, j]) for j in range(STEPS)] + [jnp.zeros((2,), jnp.float32)]
    mods = modulation(jnp.concatenate([jnp.zeros((1,), jnp.float32)] + sigmas[:STEPS]), time_proj)
    step_mods = [mods[1 + 2 * j : 3 + 2 * j] for j in range(STEPS)]
    hidden = modulate(noisy_both, step_mods[0][:, :width], step_mods[0][:, width : 2 * width])
    latent = mine(noisy_both, 1)
    values = mine(hidden, 1)

    before_both = in_order(before, swap_core(before), 0)
    past_clean = jnp.concatenate([before_both, jnp.where(is_low, clean, others)], axis=0)
    past_hidden = modulate(past_clean, mods[:1, :width], mods[:1, width : 2 * width])
    past_values = mine(past_hidden, 1)
    stack = jnp.concatenate([hidden, past_hidden], axis=0)
    stack = stack.reshape(stack.shape[0], len(plane_ids), -1).swapaxes(0, 1)
    places = jnp.stack(plane_ids + [place, core]).astype(jnp.int32)

    factors = [
        (sigmas[j + 1] - sigmas[j])[:, None] * mine(step_mods[j][:, 2 * width :], 1)
        for j in range(STEPS)
    ]
    gains = (mine(q_gain, 0)[None, :], mine(k_gain, 0)[None, :])
    spans = jnp.maximum(first_span - 2 + jnp.arange(4, dtype=jnp.int32), 0)
    segments = seg_ids[spans]
    starts = jnp.sum((seg_ids[None, :] < segments[:, None]).astype(jnp.int32), axis=1)
    positions = (
        (spans - starts)[:, None] * rows + jnp.arange(rows, dtype=jnp.int32)[None, :]
    ).astype(jnp.float32).reshape(-1, 1)
    angles = positions * frequencies(HEAD_DIM // 2)[None, :]
    cosine = jnp.concatenate([jnp.cos(angles)] * 2, axis=1)
    sine = jnp.concatenate([-jnp.sin(angles), jnp.sin(angles)], axis=1)
    tables = (cosine, sine)
    block = jnp.arange(5 * rows, dtype=jnp.int32)[None, :] // rows
    here = jnp.arange(2, dtype=jnp.int32)[:, None]
    usable = block == here
    for lag in range(1, LAGS + 1):
        allowed = (
            (first_span + here >= lag)
            & (segments[2 - lag : 4 - lag] == segments[2:])[:, None]
            & (lags_both[:, lag - 1 : lag] == 1)
        )
        usable = usable | (allowed & (block == here + 4 - lag))
    usable = usable.astype(jnp.float32)

    chips = 4 if len(pieces) == 4 else 1
    sums, planes = [], []
    for step, parts in enumerate(pieces):
        final = rests if step + 1 == len(pieces) else []
        plane, *sums = absorb(step, places, stack, parts, spots[step], chips, 2 * rows, sums, final)
        planes.append(plane)
    raw, past_raw, sums = sums
    latent, past_key = attend(
        True, inner, raw, sums, swap_core(sums), gains, tables, (usable, values, past_values),
        latent, factors[0], past_raw,
    )
    raw, sums, values = project_latent(places, latent, swap_core(latent), mods, planes, rests)
    (latent,) = attend(
        False, inner, raw, sums, swap_core(sums), gains, tables, (usable, values, past_values),
        latent, factors[1], past_key,
    )
    kept = lax.dynamic_slice_in_dim(latent, core * rows, rows, 0)
    sent = lax.dynamic_slice_in_dim(latent, (1 - core) * rows, rows, 0)
    return in_order(kept, swap_core(sent), 1)


def solution(mesh):
    placed = (
        P(("pool", "fsdp"), None),
        P(("pool", "fsdp"), None),
        P("pool"),
        P(("pool", "fsdp"), None),
        P(("pool", "fsdp"), None),
        P("fsdp", None),
        P("fsdp", None),
        P(),
        P(),
        P(),
    )
    return jax.shard_map(
        denoise, mesh=mesh, in_specs=placed, out_specs=P(("pool", "fsdp"), None), check_vma=False
    )
```

```python
import functools
import math

import jax
import jax.numpy as jnp
from jax import lax
from jax.experimental import pallas as pl
from jax.experimental.pallas import tpu as pltpu
from jax.sharding import PartitionSpec as P


HEAD_DIM = 128
STEPS = 2
LAGS = 2
LEVELS = 1000

SIGMA_SHIFT = 5.0
EPSILON = 1e-06
MASKED = -1e30
AXIS = "fsdp"


def sigma_of(levels):
    fraction = levels.astype(jnp.float32) / LEVELS
    return SIGMA_SHIFT * fraction / (1.0 + (SIGMA_SHIFT - 1.0) * fraction)


def frequencies(half_count):
    return jnp.exp(-math.log(10000.0) * jnp.arange(half_count, dtype=jnp.float32) / half_count)


def modulation(sigmas, time_proj):
    half_count = time_proj.shape[0] // 2
    angles = 1000.0 * sigmas[:, None] * frequencies(half_count)[None, :]
    features = jnp.concatenate([jnp.cos(angles), jnp.sin(angles)], axis=1).astype(jnp.bfloat16)
    return jnp.dot(features, time_proj, preferred_element_type=jnp.float32)


def modulate(latent, shift, scale):
    parts = shift.shape[0]
    values = latent.astype(jnp.float32).reshape(parts, -1, latent.shape[1])
    centred = values - jnp.mean(values, axis=-1, keepdims=True)
    variance = jnp.mean(centred * centred, axis=-1, keepdims=True)
    normed = centred * lax.rsqrt(variance + EPSILON)
    result = normed * (1.0 + scale[:, None, :]) + shift[:, None, :]
    return result.astype(jnp.bfloat16).reshape(latent.shape)


def permute(value, target_of):
    pairs = [(s, target_of(s)) for s in range(lax.axis_size(AXIS))]
    return lax.ppermute(value, AXIS, [(s, t) for s, t in pairs if t is not None])


def swap_core(value):
    return permute(value, lambda s: s ^ 1)


def swap_x(value):
    return permute(value, lambda s: s ^ 2)


def swap_y(value):
    return permute(value, lambda s: s ^ 4)


def swap_z_pair(value):
    return permute(value, lambda s: s ^ 8)


def swap_z_middle(value):
    return permute(value, lambda s: {1: s + 8, 2: s - 8}.get(s // 8))


def z_outward(value):
    return permute(value, lambda s: {1: s - 8, 2: s + 8}.get(s // 8))


def across_plane(value):
    half = value.shape[0] // 2
    from_x = swap_x(value)
    from_y = swap_y(value)
    low, high = from_x[:half], from_y[half:]
    return [value, from_x, from_y, swap_y(low), swap_x(high)]


def across_plane_in_halves(value):
    half = value.shape[0] // 2
    low, high = value[:half], value[half:]
    low_x = swap_x(low)
    high_y = swap_y(high)
    high_x = swap_x(high)
    low_y = swap_y(low)
    return [value, low_x, high_x, low_y, high_y, swap_y(low_x), swap_x(high_y)]


def gather_block(unit, device):
    z = device // 8
    place = (device // 2) % 4
    middle = (z == 1) | (z == 2)
    pair = swap_z_pair(unit)
    across = swap_z_middle(unit)
    two_mid = swap_z_middle(pair)
    two_end = z_outward(across)
    second = jnp.where(middle, two_mid, two_end)
    three_end = z_outward(second)
    third = jnp.where(middle, across, three_end)
    slots = [unit, pair, second, third]
    pieces = [across_plane(slot) for slot in slots[:3]]
    pieces.append(across_plane_in_halves(third))
    rows = unit.shape[0]
    halves = [[(i, 0, rows // 2), (i, rows // 2, rows // 2)] for i in range(4)]
    spots = [[(0, 0, rows), (1, 0, rows), (2, 0, rows)] + halves[3]] * 3
    spots.append([(0, 0, rows)] + halves[1] + halves[2] + halves[3])
    return [z ^ step for step in range(4)], place, pieces, spots


def gather_rest(unit, device):
    z = device // 8
    place = (device // 2) % 4
    middle = (z == 1) | (z == 2)
    half = unit.shape[0] // 2
    from_x = swap_x(unit)
    from_y = swap_y(unit)
    low, high = from_x[:half], from_y[half:]
    low, high = swap_y(low), swap_x(high)
    plane = jnp.zeros((4,) + unit.shape, unit.dtype)
    far = jnp.concatenate([low, high], axis=0)
    for piece, at in ((unit, place), (from_x, place ^ 1), (from_y, place ^ 2), (far, place ^ 3)):
        plane = lax.dynamic_update_slice(plane, piece[None], (at, 0, 0))
    plane = plane.reshape(-1, unit.shape[1])
    pair = swap_z_pair(plane)
    across = swap_z_middle(plane)
    two_mid = swap_z_middle(pair)
    two_end = z_outward(across)
    second = jnp.where(middle, two_mid, two_end)
    three_end = z_outward(second)
    return [plane, pair, second, across, three_end]


def gather_any(unit, device):
    size = lax.axis_size(AXIS)
    groups = [list(range(core, size, 2)) for core in range(2)]
    whole = lax.all_gather(unit, AXIS, axis=0, tiled=True, axis_index_groups=groups)
    none = jnp.int32(0)
    return [none], none, [[whole]], [[(0, 0, whole.shape[0])]]


def gather_rest_any(unit, device):
    return gather_any(unit, device)[2][0]


def begin_choice(middle, first, second, target, sem):
    inner = pltpu.make_async_copy(first, target, sem)
    outer = pltpu.make_async_copy(second, target, sem)

    @pl.when(middle)
    def _():
        inner.start()

    @pl.when(jnp.logical_not(middle))
    def _():
        outer.start()

    return inner


def absorb_body(spots, step, has_sum, rest_count, places_ref, hidden_ref, *refs):
    count = len(spots)
    piece_refs, refs = refs[:count], refs[count:]
    if has_sum:
        raw_in_ref, past_in_ref, *refs = refs
    rest_refs, refs = refs[:rest_count], refs[rest_count:]
    plane_out_ref, raw_ref, past_ref, *refs = refs
    if rest_count:
        sum_ref, plane_ref, sems, out_sem, rest_ref, rest_sems = refs
    else:
        plane_ref, sems, out_sem = refs
    place = places_ref[places_ref.shape[0] - 2]
    copies = []
    for i, (other, start, size) in enumerate(spots):
        target = plane_ref.at[jnp.bitwise_xor(place, other), pl.ds(start, size), :]
        copies.append(pltpu.make_async_copy(piece_refs[i], target, sems.at[i]))
    planes = rest_ref.shape[0] if rest_count else 0
    plain = planes - 1 if rest_count > planes else planes
    rest_copies = [
        pltpu.make_async_copy(rest_refs[i], rest_ref.at[i], rest_sems.at[i]) for i in range(plain)
    ]
    for copy in copies + rest_copies:
        copy.start()
    if plain < planes:
        middle = (places_ref[0] == 1) | (places_ref[0] == 2)
        rest_copies.append(
            begin_choice(
                middle, rest_refs[plain], rest_refs[planes], rest_ref.at[plain], rest_sems.at[plain]
            )
        )
    rows = raw_ref.shape[0]

    def multiply(index, weights):
        split = weights.shape[1] // 2
        hidden = hidden_ref[places_ref[index]]
        query = jnp.dot(hidden[:rows], weights[:, :split], preferred_element_type=jnp.float32)
        keys = jnp.dot(hidden, weights[:, split:], preferred_element_type=jnp.float32)
        return query, keys[:rows], keys[rows:]

    for copy in copies:
        copy.wait()
    out = pltpu.make_async_copy(plane_ref, plane_out_ref, out_sem)
    out.start()
    main = multiply(step, plane_ref[...].reshape(-1, plane_ref.shape[2]))
    split = main[0].shape[1]
    if has_sum:
        before = raw_in_ref[:, :split], raw_in_ref[:, split:], past_in_ref[...]
        main = [part + other for part, other in zip(main, before)]
    if rest_count:
        rest = None
        for i, copy in enumerate(rest_copies):
            copy.wait()
            parts = multiply(i, rest_ref[i])
            rest = parts if rest is None else [x + y for x, y in zip(rest, parts)]
        more = rest[0].shape[1]
    else:
        rest, more = [None] * 3, 0
    at = 0
    targets = (raw_ref, 0), (raw_ref, split + more), (past_ref, 0)
    for (target, start), part, other in zip(targets, main, rest):
        target[:, start : start + split] = part
        if rest_count:
            target[:, start + split : start + split + more] = other
            total = jnp.sum(part * part, -1, keepdims=True)
            total = total + jnp.sum(other * other, -1, keepdims=True)
            size = total.shape[0]
            sum_ref[at : at + size] = jnp.broadcast_to(total, (size, HEAD_DIM))
            at += size
    out.wait()


def absorb(step, places, hidden, pieces, spots, chips, rows, sums, rests):
    hbm = pl.BlockSpec(memory_space=pltpu.HBM)
    vmem = pl.BlockSpec(memory_space=pltpu.VMEM)
    width = pieces[0].shape[1]
    more = rests[0].shape[1] if rests else 0
    chip_rows = hidden.shape[2] // chips
    past_rows = hidden.shape[1] - rows
    operands = [places, hidden, *pieces, *sums, *rests]
    specs = [pl.BlockSpec(memory_space=pltpu.SMEM), vmem] + [hbm] * len(pieces)
    specs += [vmem] * len(sums) + [hbm] * len(rests)
    shapes = [
        pltpu.HBM((chips, chip_rows, width), jnp.bfloat16),
        jax.ShapeDtypeStruct((rows, width + more), jnp.float32),
        jax.ShapeDtypeStruct((past_rows, (width + more) // 2), jnp.float32),
    ]
    outs = [hbm, vmem, vmem]
    scratch = [
        pltpu.VMEM((chips, chip_rows, width), jnp.bfloat16),
        pltpu.SemaphoreType.DMA((len(pieces),)),
        pltpu.SemaphoreType.DMA,
    ]
    if rests:
        shapes.append(jax.ShapeDtypeStruct((2 * rows + past_rows, HEAD_DIM), jnp.float32))
        outs.append(vmem)
        scratch.append(pltpu.VMEM((hidden.shape[0],) + rests[0].shape, jnp.bfloat16))
        scratch.append(pltpu.SemaphoreType.DMA((hidden.shape[0],)))
    return pl.pallas_call(
        functools.partial(absorb_body, spots, step, bool(sums), len(rests)),
        in_specs=specs,
        out_specs=outs,
        out_shape=shapes,
        scratch_shapes=scratch,
        compiler_params=pltpu.CompilerParams(vmem_limit_bytes=16 << 20),
        name="absorb",
    )(*operands)


def turn(values, cosine, sine):
    return values * cosine + pltpu.roll(values, HEAD_DIM // 2, 1) * sine


def attend_body(first, inner, *refs):
    (raw_ref, own_sum_ref, other_sum_ref, q_gain_ref, k_gain_ref, cos_ref, sin_ref,
     usable_ref, v_ref, past_v_ref, latent_ref, factor_ref, *refs) = refs
    if first:
        past_ref, out_ref, past_key_ref = refs
    else:
        past_key_ref, out_ref = refs
    rows, width = latent_ref.shape
    extra = past_v_ref.shape[0]
    heads = width // HEAD_DIM
    scale = lax.rsqrt((own_sum_ref[...] + other_sum_ref[...]) / inner + EPSILON)
    q_scale, k_scale = scale[:rows], scale[rows : 2 * rows]
    turned = slice(extra - rows // 2, extra + rows // 2)
    own_cos, own_sin = cos_ref[turned, :], sin_ref[turned, :]

    def per_row(pair):
        rows_of = [jnp.broadcast_to(pair[i : i + 1], (rows // 2, pair.shape[1])) for i in range(2)]
        return jnp.concatenate(rows_of, axis=0)

    allowed = per_row(usable_ref[...]) > 0.0
    for head in range(heads):
        at = slice(head * HEAD_DIM, (head + 1) * HEAD_DIM)
        key_at = slice(width + at.start, width + at.stop)
        query = raw_ref[:, at] * q_scale * q_gain_ref[:, at]
        query = turn(query, own_cos, own_sin).astype(jnp.bfloat16)
        key = raw_ref[:, key_at] * k_scale * k_gain_ref[:, at]
        key = turn(key, own_cos, own_sin).astype(jnp.bfloat16)
        if first:
            past = past_ref[:, at] * scale[2 * rows :] * k_gain_ref[:, at]
            past = turn(past, cos_ref[:extra, :], sin_ref[:extra, :]).astype(jnp.bfloat16)
            past_key_ref[:, at] = past
        else:
            past = past_key_ref[:, at]
        keys = jnp.concatenate([key, past], axis=0)
        values = jnp.concatenate([v_ref[:, at], past_v_ref[:, at]], axis=0)
        scores = lax.dot_general(
            query, keys, (((1,), (1,)), ((), ())), preferred_element_type=jnp.float32
        ) * HEAD_DIM ** (-0.5)
        scores = jnp.where(allowed, scores, MASKED)
        expanded = jnp.exp(scores - jnp.max(scores, axis=-1, keepdims=True))
        weights = (expanded / jnp.sum(expanded, axis=-1, keepdims=True)).astype(jnp.bfloat16)
        mixed = jnp.dot(weights, values, preferred_element_type=jnp.float32).astype(jnp.bfloat16)
        step = per_row(factor_ref[:, at]) * mixed.astype(jnp.float32)
        out_ref[:, at] = (latent_ref[:, at].astype(jnp.float32) + step).astype(jnp.bfloat16)


def attend(first, inner, raw, sums, others, gains, tables, fixed, latent, factor, past):
    shapes = [jax.ShapeDtypeStruct(latent.shape, jnp.bfloat16)]
    if first:
        shapes.append(pltpu.HBM(past.shape, jnp.bfloat16))
    else:
        own_values, past_values = fixed[1:]
        raw, past, own_values, sums, others = (
            pltpu.with_memory_space_constraint(x, pltpu.HBM)
            for x in (raw, past, own_values, sums, others)
        )
        fixed = (fixed[0], own_values, past_values)
    return pl.pallas_call(
        functools.partial(attend_body, first, inner),
        out_shape=shapes,
        compiler_params=pltpu.CompilerParams(vmem_limit_bytes=16 << 20),
        name="attend",
    )(raw, sums, others, *gains, *tables, *fixed, latent, factor, past)


def project_body(places_ref, own_ref, other_ref, mod_ref, *refs):
    raw_ref, sum_ref, value_ref, hidden_ref, main_ref, rest_ref, sems = refs[-7:]
    count = main_ref.shape[0]
    plain = count - 1 if len(refs) - 7 > 2 * count else count
    rows, half = own_ref.shape
    parts, _, part_width = hidden_ref.shape
    copies = [pltpu.make_async_copy(refs[i], main_ref.at[i], sems.at[i]) for i in range(count)]
    copies += [
        pltpu.make_async_copy(refs[count + i], rest_ref.at[i], sems.at[count + i])
        for i in range(plain)
    ]
    for copy in copies:
        copy.start()
    if plain < count:
        middle = (places_ref[0] == 1) | (places_ref[0] == 2)
        candidates = refs[count + plain], refs[count + plain + 1]
        copies.append(
            begin_choice(middle, *candidates, rest_ref.at[plain], sems.at[count + plain])
        )
    is_low = places_ref[count + 1] == 0
    own, other = own_ref[...].astype(jnp.float32), other_ref[...].astype(jnp.float32)
    low, high = jnp.where(is_low, own, other), jnp.where(is_low, other, own)
    width = 2 * half
    mean = (jnp.sum(low, -1, keepdims=True) + jnp.sum(high, -1, keepdims=True)) / width
    low, high = low - mean, high - mean
    variance = (
        jnp.sum(low * low, -1, keepdims=True) + jnp.sum(high * high, -1, keepdims=True)
    ) / width
    scale = lax.rsqrt(variance + EPSILON)
    sides = []
    for side, centred in enumerate((low, high)):
        normed = centred * scale
        at = slice(side * half, (side + 1) * half)
        gain_at = slice(width + side * half, width + (side + 1) * half)
        pieces = []
        for span in range(2):
            piece = normed[span * (rows // 2) : (span + 1) * (rows // 2)]
            row = slice(3 + span, 4 + span)
            pieces.append(piece * (1.0 + mod_ref[row, gain_at]) + mod_ref[row, at])
        sides.append(jnp.concatenate(pieces, axis=0).astype(jnp.bfloat16))
    value_ref[...] = jnp.where(is_low, sides[0], sides[1])
    for i in range(parts):
        for side in range(2):
            if parts == 1:
                hidden_ref[0, :, side * half : (side + 1) * half] = sides[side]
            elif i * part_width // half == side:
                at = i * part_width - side * half
                hidden_ref[i] = sides[side][:, at : at + part_width]
    squares = [None, None]
    start = 0
    for weight_ref, waits in ((main_ref, copies[:count]), (rest_ref, copies[count:])):
        total = None
        for i, copy in enumerate(waits):
            copy.wait()
            weights = weight_ref[i].reshape(-1, weight_ref.shape[-1])
            part = jnp.dot(hidden_ref[places_ref[i]], weights, preferred_element_type=jnp.float32)
            total = part if total is None else total + part
        split = total.shape[1] // 2
        for i in range(2):
            side = total[:, i * split : (i + 1) * split]
            raw_ref[:, i * half + start : i * half + start + split] = side
            square = jnp.sum(side * side, -1, keepdims=True)
            squares[i] = square if squares[i] is None else squares[i] + square
        start += split
    for i in range(2):
        sum_ref[i * rows : (i + 1) * rows] = jnp.broadcast_to(squares[i], (rows, HEAD_DIM))


def project_latent(places, own, other, mods, planes, rests):
    rows, half = own.shape
    count = len(planes)
    planes, rests = (
        [pltpu.with_memory_space_constraint(plane, pltpu.HBM) for plane in group]
        for group in (planes, rests)
    )
    vmem = pl.BlockSpec(memory_space=pltpu.VMEM)
    hbm = pl.BlockSpec(memory_space=pltpu.HBM)
    return pl.pallas_call(
        project_body,
        in_specs=[pl.BlockSpec(memory_space=pltpu.SMEM)] + [vmem] * 3 + [hbm] * (count + len(rests)),
        out_shape=[
            pltpu.HBM((rows, 2 * half), jnp.float32),
            pltpu.HBM((2 * rows, HEAD_DIM), jnp.float32),
            pltpu.HBM((rows, half), jnp.bfloat16),
        ],
        scratch_shapes=[
            pltpu.VMEM((count, rows, 2 * half // count), jnp.bfloat16),
            pltpu.VMEM((count,) + planes[0].shape, jnp.bfloat16),
            pltpu.VMEM((count,) + rests[0].shape, jnp.bfloat16),
            pltpu.SemaphoreType.DMA((2 * count,)),
        ],
        compiler_params=pltpu.CompilerParams(vmem_limit_bytes=24 << 20),
        name="project",
    )(places, own, other, mods, *planes, *rests)


def denoise(noisy, clean, seg_ids, lag_mask, plan, w_query, w_key, time_proj, q_gain, k_gain):
    rows, width = noisy.shape
    inner = w_query.shape[1]
    half = inner // 2
    devices = lax.axis_size(AXIS)
    device = lax.axis_index(AXIS)
    core = device % 2
    first_span = device - core
    is_low = core == 0

    def mine(value, axis):
        return lax.dynamic_slice_in_dim(value, core * half, half, axis)

    def in_order(own, other, axis):
        low = jnp.where(is_low, own, other)
        high = jnp.where(is_low, other, own)
        return jnp.concatenate([low, high], axis=axis)

    before = permute(clean, lambda s: s + 2 if s + 2 < devices else None)
    others = swap_core(clean)

    split = (half // HEAD_DIM) * 4 // 5 * HEAD_DIM

    def columns(start, low, high):
        return jnp.concatenate(
            [lax.dynamic_slice_in_dim(w, start + low, high - low, 1) for w in (w_query, w_key)],
            axis=1,
        )

    own_start, other_start = core * half, (1 - core) * half
    unit = in_order(
        columns(own_start, 0, split), swap_core(columns(other_start, 0, split)), 0
    )
    sent_rest = swap_core(columns(other_start, split, half))
    rest_unit = in_order(columns(own_start, split, half), sent_rest, 0)
    unit, noisy, seg_ids, plan, lag_mask, time_proj = lax.optimization_barrier(
        (unit, noisy, seg_ids, plan, lag_mask, time_proj)
    )
    on_block = devices == 32
    plane_ids, place, pieces, spots = (gather_block if on_block else gather_any)(unit, device)
    rests = (gather_rest if on_block else gather_rest_any)(rest_unit, device)
    noisy_both = in_order(noisy, swap_core(noisy), 0)
    small = jnp.concatenate([plan, lag_mask], axis=1)
    small_both = in_order(small, swap_core(small), 0)
    plan_both, lags_both = small_both[:, :STEPS], small_both[:, STEPS:]
    sigmas = [sigma_of(plan_both[:, j]) for j in range(STEPS)] + [jnp.zeros((2,), jnp.float32)]
    mods = modulation(jnp.concatenate([jnp.zeros((1,), jnp.float32)] + sigmas[:STEPS]), time_proj)
    step_mods = [mods[1 + 2 * j : 3 + 2 * j] for j in range(STEPS)]
    hidden = modulate(noisy_both, step_mods[0][:, :width], step_mods[0][:, width : 2 * width])
    latent = mine(noisy_both, 1)
    values = mine(hidden, 1)

    before_both = in_order(before, swap_core(before), 0)
    past_clean = jnp.concatenate([before_both, jnp.where(is_low, clean, others)], axis=0)
    past_hidden = modulate(past_clean, mods[:1, :width], mods[:1, width : 2 * width])
    past_values = mine(past_hidden, 1)
    stack = jnp.concatenate([hidden, past_hidden], axis=0)
    stack = stack.reshape(stack.shape[0], len(plane_ids), -1).swapaxes(0, 1)
    places = jnp.stack(plane_ids + [place, core]).astype(jnp.int32)

    factors = [
        (sigmas[j + 1] - sigmas[j])[:, None] * mine(step_mods[j][:, 2 * width :], 1)
        for j in range(STEPS)
    ]
    gains = (mine(q_gain, 0)[None, :], mine(k_gain, 0)[None, :])
    spans = jnp.maximum(first_span - 2 + jnp.arange(4, dtype=jnp.int32), 0)
    segments = seg_ids[spans]
    starts = jnp.sum((seg_ids[None, :] < segments[:, None]).astype(jnp.int32), axis=1)
    positions = (
        (spans - starts)[:, None] * rows + jnp.arange(rows, dtype=jnp.int32)[None, :]
    ).astype(jnp.float32).reshape(-1, 1)
    angles = positions * frequencies(HEAD_DIM // 2)[None, :]
    cosine = jnp.concatenate([jnp.cos(angles)] * 2, axis=1)
    sine = jnp.concatenate([-jnp.sin(angles), jnp.sin(angles)], axis=1)
    tables = (cosine, sine)
    block = jnp.arange(5 * rows, dtype=jnp.int32)[None, :] // rows
    here = jnp.arange(2, dtype=jnp.int32)[:, None]
    usable = block == here
    for lag in range(1, LAGS + 1):
        allowed = (
            (first_span + here >= lag)
            & (segments[2 - lag : 4 - lag] == segments[2:])[:, None]
            & (lags_both[:, lag - 1 : lag] == 1)
        )
        usable = usable | (allowed & (block == here + 4 - lag))
    usable = usable.astype(jnp.float32)

    chips = 4 if len(pieces) == 4 else 1
    sums, planes = [], []
    for step, parts in enumerate(pieces):
        final = rests if step + 1 == len(pieces) else []
        plane, *sums = absorb(step, places, stack, parts, spots[step], chips, 2 * rows, sums, final)
        planes.append(plane)
    raw, past_raw, sums = sums
    latent, past_key = attend(
        True, inner, raw, sums, swap_core(sums), gains, tables, (usable, values, past_values),
        latent, factors[0], past_raw,
    )
    raw, sums, values = project_latent(places, latent, swap_core(latent), mods, planes, rests)
    (latent,) = attend(
        False, inner, raw, sums, swap_core(sums), gains, tables, (usable, values, past_values),
        latent, factors[1], past_key,
    )
    kept = lax.dynamic_slice_in_dim(latent, core * rows, rows, 0)
    sent = lax.dynamic_slice_in_dim(latent, (1 - core) * rows, rows, 0)
    other = swap_core(sent)
    joined = jnp.concatenate([kept, other, kept], axis=1)
    return lax.dynamic_slice_in_dim(joined, core * half, width, 1)


def solution(mesh):
    placed = (
        P(("pool", "fsdp"), None),
        P(("pool", "fsdp"), None),
        P("pool"),
        P(("pool", "fsdp"), None),
        P(("pool", "fsdp"), None),
        P("fsdp", None),
        P("fsdp", None),
        P(),
        P(),
        P(),
    )
    return jax.shard_map(
        denoise, mesh=mesh, in_specs=placed, out_specs=P(("pool", "fsdp"), None), check_vma=False
    )
```
